32 devices in a mesh: grp: 2 (over x), probe: 8 (over z, y), beam: 2 (over core).
Axes of the slice: x: 2, y: 2, z: 4, core: 2. Of those that a mesh axis runs over, the one named last changes fastest.
Arguments:
- smatrix: bfloat16 [8192, 8, 512], P(('grp', 'beam'), 'probe'), parts along dimension 0, may hold values from -0.09375 to 0.09375
- aperture: float32 [4096], P('beam'), may hold values from 0.5 to 1.5
- aberration: float32 [4096], P('beam'), may hold values from -3.140625 to 3.140625
- beam_k: int32 [2, 4096], P(None, 'beam'), may hold values from -32 to 31, as said below
- probe_pos: int32 [2, 2048], P(None, 'probe'), may hold values from 0 to 1023
- patches: bfloat16 [128, 512], P(('grp', 'probe')), parts along dimension 0, may hold values from -6 to 6
- patch_col: int32 [128], P('grp'), parts along dimension 0, may hold values from 0 to 7, never falling along the last dimension, each value on 1 to 32 neighbouring positions
Outputs:
- ionization: float32 [16, 2048], P('grp', ('probe', 'beam')), parts along dimension 0
The draws below stay inside these ranges and needn't reach their ends.
There are 2 independent parts, one for each index of `grp`. The reference program is written for one: setup_inputs(seed, part) draws one part's arguments, and reference() takes and returns one part's arrays. A program takes and returns all parts, laid end to end along the dimension named above; an argument that names none is the same for every part. Nothing has to cross between parts.
Inputs may be any that keep to these rules, and one draw needn't show every extreme that they name: `patch_col`: patches are ordered by atom column; each of the 8 columns has 1 to 32 patches, and some column has exactly 32. `beam_k`: no two beams have the same pair of indices.
All inputs are finite; a program needn't handle non-finite values.
Results may differ from the reference program's by a relative error of at most 0.005.
Values may be sent and summed in bfloat16 or wider, within the bound.
A program may use at most 128 MiB of HBM per device.

```python
import math
import jax
import jax.numpy as jnp
import numpy as np
from jax import lax

NB = 4096
PSIDE = 16
PIX = 256
GRID = 1024
KMAX = 32
NCOL = 8
NPATCH = 64
MOSTP = 32
PTOT = 2048


def draw_beam_k(key, part):
    side_count = 2 * KMAX
    total_points = side_count * side_count
    rank_score = jax.random.permutation(jax.random.fold_in(key, 11), total_points).astype(jnp.int32) + 2
    grid_index = jnp.arange(total_points, dtype=jnp.int32)
    rank_score = jnp.where(grid_index == 0, 0, rank_score)
    rank_score = jnp.where(grid_index == total_points - 1, 1, rank_score)
    chosen_points = jnp.argsort(rank_score, stable=True)[:NB].astype(jnp.int32)
    shuffled = jax.random.permutation(jax.random.fold_in(key, 23), chosen_points).astype(jnp.int32)
    first_index = shuffled // side_count - KMAX
    second_index = shuffled % side_count - KMAX
    return jnp.stack([first_index, second_index]).astype(jnp.int32)


def touch_ends(values, own_key, low, largest):
    place = [jax.random.randint(jax.random.fold_in(own_key, axis), (), 0, length) for axis, length in enumerate(values.shape)]
    main_axis = values.shape.index(max(values.shape))
    neighbour = place[:main_axis] + [(place[main_axis] + 1) % values.shape[main_axis]] + place[main_axis + 1:]
    return values.at[tuple(place)].set(low).at[tuple(neighbour)].set(largest)


def levels(rng, extent, cuts, low, high):
    level, own = 1.0, jax.random.fold_in(rng, 6)
    for position, shards_of in cuts:
        heights = jnp.exp(jax.random.uniform(jax.random.fold_in(own, position), (shards_of,), jnp.float32, low / len(cuts), high / len(cuts)))
        level = level * jnp.repeat(heights, extent[position] // shards_of).reshape([-1 if axis == position else 1 for axis in range(len(extent))])
    return level


def split_up(number_of, total, most, skew):
    weights = [(1 << 20) // math.isqrt(rank ** skew) + 1 for rank in range(2, number_of + 1)]
    spare, counts = total - most - (number_of - 1), [1] * (number_of - 1)
    while spare > 0:
        free = [i for i in range(number_of - 1) if counts[i] < most]
        whole, remaining = sum([weights[i] for i in free]), spare
        for i in free:
            extra = min(most - counts[i], max(1, remaining * weights[i] // whole), spare)
            counts[i] = counts[i] + extra
            spare = spare - extra
    return np.array([most] + counts)


def ragged_sizes(own_key, count, total, limit, skew):
    if count == 2:
        one = jax.random.randint(own_key, (), max(1, total - limit), min(limit, total - 1) + 1)
        return jnp.stack([one, total - one])
    lengths = jnp.asarray(split_up(count, total, limit, skew), jnp.int32)
    pairs = (count - 1) // 2
    giver, receiver = lengths[1:1 + 2 * pairs:2], lengths[2:2 + 2 * pairs:2]
    margin = jnp.minimum(giver - 1, limit - receiver)
    moved = jax.random.randint(jax.random.fold_in(own_key, 1), (pairs,), 0, 1 << 20) % (margin + 1)
    lengths = lengths.at[1:1 + 2 * pairs:2].set(giver - moved).at[2:2 + 2 * pairs:2].set(receiver + moved)
    return lengths[jax.random.permutation(jax.random.fold_in(own_key, 2), count)]


def bell_draw(stream_key, shape, deviation, most, pieces=(), kind=jnp.bfloat16):
    factor_of = levels(stream_key, shape, pieces, -0.22, 0.18) if pieces else 1.0
    values = jax.random.normal(stream_key, shape, jnp.float32) * deviation * factor_of
    return jnp.minimum(jnp.maximum(values, -most), most).astype(kind)


def setup_inputs(seed: int = 0, part: int = 0) -> dict:
    arg_keys = jax.random.split(jax.random.key(seed), 8)
    part_keys = jax.random.split(jax.random.fold_in(arg_keys[7], part), 8)
    smatrix = bell_draw(part_keys[0], (NB, NCOL, 2 * PIX), NB ** -0.5, 0.09375, ((0, 2), (1, 8)))
    aperture = jnp.clip(0.5 + 1.0 * jax.random.uniform(arg_keys[1], (NB,), jnp.float32) ** levels(arg_keys[1], (NB,), ((0, 2),), -0.2, 0.2), 0.5, 1.5)
    aberration = jnp.clip(jax.random.uniform(arg_keys[2], (NB,), jnp.float32, -3.140625, 3.140625), -3.140625, 3.140625)
    beam_k = draw_beam_k(jax.random.fold_in(arg_keys[7], 71), part)
    probe_pos = touch_ends(jax.random.randint(arg_keys[4], (2, PTOT), 0, GRID), jax.random.fold_in(arg_keys[4], 1), 0, GRID - 1).astype(jnp.int32)
    patches = bell_draw(part_keys[5], (NPATCH, 2 * PIX), 1.0, 6.0, ((0, 8),))
    patch_col = jnp.searchsorted(jnp.cumsum(ragged_sizes(part_keys[6], NCOL, NPATCH, MOSTP, 2)), jnp.arange(NPATCH), side="right").astype(jnp.int32)
    return dict(smatrix=smatrix, aperture=aperture, aberration=aberration, beam_k=beam_k, probe_pos=probe_pos, patches=patches, patch_col=patch_col)


def coefficients(beam_k, aperture, aberration, positions):
    turn_count = jnp.mod(positions[0][:, None] * beam_k[0][None, :] + positions[1][:, None] * beam_k[1][None, :], GRID)
    phase_angle = aberration[None, :] + (2.0 * math.pi / GRID) * turn_count.astype(jnp.float32)
    real_coef = (aperture[None, :] * jnp.cos(phase_angle)).astype(jnp.bfloat16)
    imag_coef = (-(aperture[None, :] * jnp.sin(phase_angle))).astype(jnp.bfloat16)
    return real_coef, imag_coef


def detector(edge_count):
    half_side = edge_count // 2
    pixel_index = jnp.arange(edge_count * edge_count, dtype=jnp.int32)
    mode_index = jnp.arange(edge_count * half_side, dtype=jnp.int32)
    row_off = pixel_index // edge_count
    col_off = pixel_index % edge_count
    freq_first = mode_index // half_side - half_side
    freq_second = mode_index % half_side - edge_count // 4
    turn_count = jnp.mod(row_off[:, None] * freq_first[None, :] + col_off[:, None] * freq_second[None, :], edge_count)
    angle_value = (2.0 * math.pi / edge_count) * turn_count.astype(jnp.float32)
    real_part = jnp.cos(angle_value)
    imag_part = -jnp.sin(angle_value)
    upper_rows = jnp.concatenate([real_part, imag_part], axis=1)
    lower_rows = jnp.concatenate([-imag_part, real_part], axis=1)
    return jnp.concatenate([upper_rows, lower_rows], axis=0).astype(jnp.bfloat16)


def patch_energy(picked, pot_rows, det_table):
    half_width = pot_rows.shape[-1] // 2
    psi_re = picked[..., :half_width].astype(jnp.float32)
    psi_im = picked[..., half_width:].astype(jnp.float32)
    pot_re = pot_rows[:, :half_width].astype(jnp.float32)
    pot_im = pot_rows[:, half_width:].astype(jnp.float32)
    wave_out = jnp.concatenate([psi_re * pot_re - psi_im * pot_im, psi_re * pot_im + psi_im * pot_re], axis=-1).astype(jnp.bfloat16)
    projected = jnp.einsum("rjx,xq->rjq", wave_out.astype(jnp.float32), det_table.astype(jnp.float32))
    return jnp.sum(projected * projected, axis=-1) / float(half_width * (det_table.shape[1] // 2))


def reference(smatrix, aperture, aberration, beam_k, probe_pos, patches, patch_col):
    det_table = detector(PSIDE)
    half_width = smatrix.shape[2] // 2
    flat_matrix = smatrix.reshape(NB, NCOL * 2 * half_width)
    block_rows = math.gcd(PTOT, 512)
    pos_blocks = probe_pos.reshape(2, PTOT // block_rows, block_rows).transpose(1, 0, 2)
    onehot = (patch_col[:, None] == jnp.arange(NCOL, dtype=jnp.int32)[None, :]).astype(jnp.float32)

    def per_block(positions):
        real_coef, imag_coef = coefficients(beam_k, aperture, aberration, positions)
        from_re = jnp.dot(real_coef, flat_matrix, preferred_element_type=jnp.float32).reshape(block_rows, NCOL, 2 * half_width)
        from_im = jnp.dot(imag_coef, flat_matrix, preferred_element_type=jnp.float32).reshape(block_rows, NCOL, 2 * half_width)
        psi = jnp.concatenate([from_re[..., :half_width] - from_im[..., half_width:], from_re[..., half_width:] + from_im[..., :half_width]], axis=-1).astype(jnp.bfloat16)
        picked = jnp.take(psi, patch_col, axis=1)
        energy = patch_energy(picked, patches, det_table)
        return jnp.dot(energy, onehot, precision=lax.Precision.HIGHEST)

    result = lax.map(per_block, pos_blocks)
    return result.reshape(PTOT, NCOL).T
```

```python
import functools
import math

import jax
import jax.numpy as jnp
import numpy as np
from jax import lax
from jax.experimental import pallas as pl
from jax.experimental.pallas import tpu as pltpu
from jax.sharding import PartitionSpec as P

PSIDE = 16
GRID = 1024
LANES = 128
ROUND = 1.5 * 2.0**23
MESH = pl.DeviceIdType.MESH


def overlap_table(edge_count):
    half_side = edge_count // 2
    pixel = np.arange(edge_count * edge_count)
    mode = np.arange(edge_count * half_side)
    first = mode // half_side - half_side
    second = mode % half_side - edge_count // 4
    turns = np.mod(
        (pixel // edge_count)[:, None] * first[None, :]
        + (pixel % edge_count)[:, None] * second[None, :],
        edge_count,
    )
    angle = np.float32(2.0 * math.pi / edge_count) * turns.astype(np.float32)
    e_re = np.cos(angle).astype(jnp.bfloat16).astype(np.float64)
    e_im = (-np.sin(angle)).astype(jnp.bfloat16).astype(np.float64)
    g_re = e_re @ e_re.T + e_im @ e_im.T
    g_im = e_im @ e_re.T - e_re @ e_im.T
    return np.stack([g_re, g_im]).astype(np.float32)


def cos_sin_turns(u):
    r = u - ((u + ROUND) - ROUND)
    x = r * r
    s = r * (4.4415360 + x * (-7.2646804 + x * 3.2520479))
    c = 1.4142041 + x * (-6.9776420 + x * (5.7152380 + x * -1.7283475))
    return 1.0 - s * s, s * c


def kernel(
    peers, s_hbm, amp_ref, aber_ref, k_ref, pos_ref, pat_ref, col_ref, g_hbm, out_ref,
    s_v, w_v, g_v, kf, pb, posbuf, patbuf, nmat, psend, pown, precv, osend, orecv,
    dma_sem, pos_ss, pos_rs, pat_ss, pat_rs, psi_ss, psi_rs, out_ss, out_rs,
    *accs,
):
    me = lax.axis_index("probe")
    core = lax.axis_index("beam")
    beams, width = s_v.shape
    pix = width // 2
    half = precv.shape[0]
    rows = min(half, 1024)
    blk = min(rows, 256)
    nblk = rows // blk
    nsub = half // rows
    groups = beams // LANES
    left, right = accs[:nblk], accs[nblk:]

    s_copy = pltpu.make_async_copy(s_hbm, s_v, dma_sem.at[0])
    g_copy = pltpu.make_async_copy(g_hbm, g_v, dma_sem.at[1])
    s_copy.start()
    g_copy.start()

    others = [lax.rem(me + step, peers) for step in range(1, peers)]
    barrier = pltpu.get_barrier_semaphore()
    for other in others:
        pl.semaphore_signal(barrier, inc=1, device_id={"probe": other}, device_id_type=MESH)
    pl.semaphore_signal(barrier, inc=1, device_id={"beam": 1 - core}, device_id_type=MESH)

    posbuf[me] = pos_ref[...]
    pat = pat_ref[...].astype(jnp.float32)
    patbuf[me] = jnp.concatenate([pat[:, :pix], pat[:, pix:]], axis=0).astype(jnp.bfloat16)
    pl.semaphore_wait(barrier, peers)

    def to_peer(buf_src, buf_dst, ss, rs, step, other):
        return pltpu.make_async_remote_copy(
            src_ref=buf_src, dst_ref=buf_dst, send_sem=ss.at[step], recv_sem=rs,
            device_id={"probe": other}, device_id_type=MESH,
        )

    pos_out, pat_out = [], []
    for step, other in enumerate(others):
        pos_out.append(to_peer(posbuf.at[me], posbuf.at[me], pos_ss, pos_rs.at[me], step, other))
        pos_out[-1].start()
    for step, other in enumerate(others):
        pat_out.append(to_peer(patbuf.at[me], patbuf.at[me], pat_ss, pat_rs.at[me], step, other))
        pat_out[-1].start()

    kf[...] = k_ref[...].astype(jnp.float32) * (1.0 / GRID)
    amp = amp_ref[...]
    aber = aber_ref[...]
    amp_cos = jnp.transpose(amp * jnp.cos(aber))
    amp_sin = jnp.transpose(amp * jnp.sin(aber))
    s_copy.wait()
    for g in range(groups):
        s_blk = s_v[g * LANES : (g + 1) * LANES, :].astype(jnp.float32)
        s_re, s_im = s_blk[:, :pix], s_blk[:, pix:]
        fc, fs = amp_cos[:, g : g + 1], amp_sin[:, g : g + 1]
        c_re = fc * s_re + fs * s_im
        c_im = fc * s_im - fs * s_re
        base = 2 * g * LANES
        w_v[base : base + LANES, :pix] = c_re.astype(jnp.bfloat16)
        w_v[base : base + LANES, pix:] = c_im.astype(jnp.bfloat16)
        w_v[base + LANES : base + 2 * LANES, :pix] = c_im.astype(jnp.bfloat16)
        w_v[base + LANES : base + 2 * LANES, pix:] = (-c_re).astype(jnp.bfloat16)

    for step, other in enumerate(others):
        to_peer(posbuf.at[other], posbuf.at[other], pos_ss, pos_rs.at[other], step, other).wait_recv()
    part = half // peers
    for d in range(peers):
        for b in range(2):
            for t in range(part // LANES):
                for axis in range(2):
                    lo = b * part + t * LANES
                    line = posbuf[d, axis : axis + 1, lo : lo + LANES].astype(jnp.float32)
                    at = b * half + d * part + t * LANES
                    pb[axis, at : at + LANES, :] = jnp.transpose(
                        jnp.broadcast_to(line, (LANES, LANES))
                    )

    def waves(first_row, dst, dst_row):
        def group(g, carry):
            cols = pl.ds(pl.multiple_of(g * LANES, LANES), LANES)
            k1, k2 = kf[0:1, cols], kf[1:2, cols]
            wrows = pl.ds(pl.multiple_of(g * 2 * LANES, 2 * LANES), 2 * LANES)
            pltpu.matmul_push_rhs(w_v[wrows, :pix], 0, 0)
            pltpu.matmul_push_rhs(w_v[wrows, pix:], 0, 1)
            for n in range(nblk):
                prow = pl.ds(pl.multiple_of(first_row + n * blk, blk), blk)
                cos_t, sin_t = cos_sin_turns(pb[0, prow, :] * k1 + pb[1, prow, :] * k2)
                lhs = jnp.concatenate(
                    [cos_t.astype(jnp.bfloat16), sin_t.astype(jnp.bfloat16)], axis=1
                )
                staged = 0 if n == 0 else None
                pltpu.matmul_acc_lhs(left[n], lhs, load_staged_rhs=staged)
                pltpu.matmul_acc_lhs(right[n], lhs, load_staged_rhs=staged)
            return carry

        lax.fori_loop(0, groups, group, 0, unroll=2)
        for n in range(nblk):
            dst[dst_row + n * blk : dst_row + (n + 1) * blk, :pix] = pltpu.matmul_pop(left[n])
            dst[dst_row + n * blk : dst_row + (n + 1) * blk, pix:] = pltpu.matmul_pop(right[n])

    psi_out = []
    for sub in range(nsub):
        waves((1 - core) * half + sub * rows, psend, sub * rows)
        span = pl.ds(sub * rows, rows)
        psi_out.append(
            pltpu.make_async_remote_copy(
                src_ref=psend.at[span], dst_ref=precv.at[span], send_sem=psi_ss.at[sub],
                recv_sem=psi_rs.at[sub], device_id={"beam": 1 - core}, device_id_type=MESH,
            )
        )
        psi_out[-1].start()

    def product(lhs, rhs):
        for lo in range(0, lhs.shape[1], pix):
            pltpu.matmul_push_rhs(rhs[lo : lo + pix, :pix], 0, 0)
            pltpu.matmul_push_rhs(rhs[lo : lo + pix, pix:], 0, 1)
            pltpu.matmul_acc_lhs(left[0], lhs[:, lo : lo + pix], load_staged_rhs=0)
            pltpu.matmul_acc_lhs(right[0], lhs[:, lo : lo + pix], load_staged_rhs=0)
        return jnp.concatenate([pltpu.matmul_pop(left[0]), pltpu.matmul_pop(right[0])], axis=1)

    for step, other in enumerate(others):
        to_peer(patbuf.at[other], patbuf.at[other], pat_ss, pat_rs.at[other], step, other).wait_recv()
    g_copy.wait()
    per = patbuf.shape[1] // 2
    p_all = patbuf[...].astype(jnp.float32)
    p_re = jnp.concatenate([p_all[d, :per] for d in range(peers)], axis=0)
    p_im = jnp.concatenate([p_all[d, per:] for d in range(peers)], axis=0)
    mine = jnp.where(col_ref[...] == me, 1.0, 0.0)
    lhs = jnp.concatenate([jnp.transpose(p_re) * mine, jnp.transpose(p_im) * mine], axis=1)
    rhs = jnp.concatenate(
        [jnp.concatenate([p_re, -p_im], axis=1), jnp.concatenate([p_im, p_re], axis=1)], axis=0
    )
    spare = -lhs.shape[1] % pix
    if spare:
        lhs = jnp.concatenate([lhs, jnp.zeros((pix, spare), jnp.float32)], axis=1)
        rhs = jnp.concatenate([rhs, jnp.zeros((spare, width), jnp.float32)], axis=0)
    lhs, rhs = lhs.astype(jnp.bfloat16), rhs.astype(jnp.bfloat16)
    q = product(lhs, rhs)
    q_re, q_im = q[:, :pix], q[:, pix:]
    g_re, g_im = g_v[0], g_v[1]
    scale = 1.0 / float(pix * (pix // 2))
    m_re = (q_re * g_re - q_im * g_im) * scale
    m_im = (q_re * g_im + q_im * g_re) * (2.0 * scale)
    for lo, m in ((0, m_re), (pix, m_im)):
        high = m.astype(jnp.bfloat16)
        nmat[0, :, lo : lo + pix] = high
        nmat[1, :, lo : lo + pix] = (m - high.astype(jnp.float32)).astype(jnp.bfloat16)

    for sub in range(nsub):
        waves(core * half + sub * rows, pown, sub * rows)
    for sub in range(nsub):
        psi_out[sub].wait_recv()
        psi = []
        for n in range(nblk):
            span = pl.ds(sub * rows + n * blk, blk)
            psi.append((pown[span, :] + precv[span, :]).astype(jnp.bfloat16))
        for term in range(2):
            pltpu.matmul_push_rhs(nmat[term, :, :pix], 0, 0)
            pltpu.matmul_push_rhs(nmat[term, :, pix:], 0, 1)
            for n in range(nblk):
                staged = 0 if n == 0 else None
                pltpu.matmul_acc_lhs(left[n], psi[n][:, :pix], load_staged_rhs=staged)
                pltpu.matmul_acc_lhs(right[n], psi[n][:, :pix], load_staged_rhs=staged)
            pltpu.matmul_push_rhs(nmat[term, :, :pix], 0, 1)
            for n in range(nblk):
                staged = 0 if n == 0 else None
                pltpu.matmul_acc_lhs(right[n], psi[n][:, pix:], load_staged_rhs=staged)
        for n in range(nblk):
            z = pltpu.matmul_pop(left[n]) * psi[n][:, :pix].astype(jnp.float32)
            z += pltpu.matmul_pop(right[n]) * psi[n][:, pix:].astype(jnp.float32)
            z = z[:, :LANES] + z[:, LANES:]
            for row in range(0, blk, LANES):
                turned = jnp.transpose(z[row : row + LANES, :])
                total = turned[0:8]
                for t in range(8, LANES, 8):
                    total += turned[t : t + 8]
                at = sub * rows + n * blk + row
                osend[at // part, :, at % part : at % part + LANES] = total

    out_sent = []
    for step, other in enumerate(others):
        out_sent.append(to_peer(osend.at[other], orecv.at[me], out_ss, out_rs.at[me], step, other))
        out_sent[-1].start()
    orecv[me] = osend[me]
    for step, other in enumerate(others):
        to_peer(osend.at[other], orecv.at[other], out_ss, out_rs.at[other], step, other).wait_recv()
    out_ref[...] = jnp.sum(orecv[...], axis=1)
    for sent in pos_out + pat_out + psi_out + out_sent:
        sent.wait_send()


def scoped_kernel(peers, rows, *refs):
    blk = min(rows, 256)
    pix = refs[0].shape[1] // 2
    accs = [pltpu.ACC(mxu)((blk, pix), jnp.float32) for mxu in (0, 1) for _ in range(rows // blk)]
    pl.run_scoped(functools.partial(kernel, peers, *refs), *accs)


def shards(smatrix, aperture, aberration, beam_k, probe_pos, patches, patch_col):
    peers = lax.axis_size("probe")
    beams, _, width = smatrix.shape
    here = probe_pos.shape[1]
    part = here // lax.axis_size("beam")
    half = peers * part
    per = patches.shape[0]
    pix = width // 2
    overlap = overlap_table(PSIDE)
    vmem = pl.BlockSpec(memory_space=pltpu.VMEM)
    hbm = pl.BlockSpec(memory_space=pl.ANY)
    f32, bf16 = jnp.float32, jnp.bfloat16
    sends = pltpu.SemaphoreType.DMA((peers - 1,))
    receipts = pltpu.SemaphoreType.DMA((peers,))
    subs = pltpu.SemaphoreType.DMA((half // min(half, 1024),))
    return pl.pallas_call(
        functools.partial(scoped_kernel, peers, min(half, 1024)),
        out_shape=jax.ShapeDtypeStruct((peers, part), f32),
        in_specs=[hbm, vmem, vmem, vmem, vmem, vmem, vmem, hbm],
        out_specs=vmem,
        scratch_shapes=[
            pltpu.VMEM((beams, width), bf16),
            pltpu.VMEM((2 * beams, width), bf16),
            pltpu.VMEM(overlap.shape, f32),
            pltpu.VMEM((2, beams), f32),
            pltpu.VMEM((2, 2 * half, LANES), f32),
            pltpu.VMEM((peers, 2, here), jnp.int32),
            pltpu.VMEM((peers, 2 * per, pix), bf16),
            pltpu.VMEM((2, pix, width), bf16),
            pltpu.VMEM((half, width), f32),
            pltpu.VMEM((half, width), f32),
            pltpu.VMEM((half, width), f32),
            pltpu.VMEM((peers, 8, part), f32),
            pltpu.VMEM((peers, 8, part), f32),
            pltpu.SemaphoreType.DMA((2,)),
            sends, receipts, sends, receipts, subs, subs, sends, receipts,
        ],
        compiler_params=pltpu.CompilerParams(
            collective_id=0, has_side_effects=True, vmem_limit_bytes=56 << 20
        ),
    )(
        smatrix.reshape(beams, width),
        aperture.reshape(beams // LANES, LANES),
        aberration.reshape(beams // LANES, LANES),
        beam_k,
        probe_pos,
        patches,
        patch_col.reshape(1, patch_col.shape[0]),
        jnp.asarray(overlap),
    )


def solution(mesh):
    placed = (
        P(("grp", "beam"), "probe", None),
        P("beam"),
        P("beam"),
        P(None, "beam"),
        P(None, "probe"),
        P(("grp", "probe"), None),
        P("grp"),
    )
    whole = jax.shard_map(
        shards, mesh=mesh, in_specs=placed, out_specs=P("grp", ("probe", "beam")), check_vma=False
    )

    def run(*args):
        with jax.sharding.use_abstract_mesh(mesh.abstract_mesh):
            return whole(*args)

    return run
```

```python
import functools
import math

import jax
import jax.numpy as jnp
import numpy as np
from jax import lax
from jax.experimental import pallas as pl
from jax.experimental.pallas import tpu as pltpu
from jax.sharding import PartitionSpec as P

PSIDE = 16
GRID = 1024
LANES = 128
ROUND = 1.5 * 2.0**23
MESH = pl.DeviceIdType.MESH


def overlap_table(edge_count):
    half_side = edge_count // 2
    pixel = np.arange(edge_count * edge_count)
    mode = np.arange(edge_count * half_side)
    first = mode // half_side - half_side
    second = mode % half_side - edge_count // 4
    turns = np.mod(
        (pixel // edge_count)[:, None] * first[None, :]
        + (pixel % edge_count)[:, None] * second[None, :],
        edge_count,
    )
    angle = np.float32(2.0 * math.pi / edge_count) * turns.astype(np.float32)
    e_re = np.cos(angle).astype(jnp.bfloat16).astype(np.float64)
    e_im = (-np.sin(angle)).astype(jnp.bfloat16).astype(np.float64)
    g_re = e_re @ e_re.T + e_im @ e_im.T
    g_im = e_im @ e_re.T - e_re @ e_im.T
    return np.stack([g_re, g_im]).astype(np.float32)


def cos_sin_turns(u):
    r = u - ((u + ROUND) - ROUND)
    x = r * r
    s = r * (4.4415360 + x * (-7.2646804 + x * 3.2520479))
    c = 1.4142041 + x * (-6.9776420 + x * (5.7152380 + x * -1.7283475))
    return 1.0 - s * s, s * c


def ring_spot(index, peers):
    if peers != 8:
        return index
    line, along = lax.rem(index, 2), index // 2
    return along * (1 - line) + (peers - 1 - along) * line


def ring_index(spot, peers):
    if peers != 8:
        return spot
    line = spot // (peers // 2)
    return 2 * spot * (1 - line) + (2 * (peers - 1 - spot) + 1) * line


def chunk_order(peers):
    far = [(d, peers - d) for d in range(peers // 2 - 1, 2, -1)]
    return [(1, peers - 1)] + far + [(0, peers // 2), (2, peers - 2)]


def kernel(
    peers, s_hbm, amp_ref, aber_ref, k_ref, pos_ref, pat_ref, col_ref, g_hbm, out_ref,
    s_v, w_v, g_v, kf, pb, posbuf, patbuf, nmat, psend, pown, precv, osend, orecv,
    s_sem, g_sem, pos_ss, pos_rs, pat_ss, pat_rs, psi_ss, psi_rs, out_ss, out_rs,
    *accs,
):
    me = lax.axis_index("probe")
    core = lax.axis_index("beam")
    beams, width = s_v.shape
    pix = width // 2
    groups = beams // LANES
    part = pos_ref.shape[1] // 2
    chunks, pair_rows = psend.shape[:2]
    left, right = accs[:2], accs[2:4]
    left_end, right_end = accs[4], accs[5]

    spot = ring_spot(me, peers)

    def at_offset(offset):
        return ring_index(lax.rem(spot + offset + peers, peers), peers)

    pieces = s_sem.shape[0]
    piece = beams // pieces
    s_copies = [
        pltpu.make_async_copy(
            s_hbm.at[pl.ds(i * piece, piece)], s_v.at[pl.ds(i * piece, piece)], s_sem.at[i]
        )
        for i in range(pieces)
    ]
    for copy in s_copies:
        copy.start()
    g_copy = pltpu.make_async_copy(g_hbm, g_v, g_sem.at[0])
    g_copy.start()

    barrier = pltpu.get_barrier_semaphore()
    for step in (1, -1):
        pl.semaphore_signal(
            barrier, inc=1, device_id={"probe": at_offset(step)}, device_id_type=MESH
        )
    pl.semaphore_signal(barrier, inc=1, device_id={"beam": 1 - core}, device_id_type=MESH)

    posbuf[0] = pos_ref[...]
    pat = pat_ref[...].astype(jnp.float32)
    patbuf[0] = jnp.concatenate([pat[:, :pix], pat[:, pix:]], axis=0).astype(jnp.bfloat16)
    kf[...] = k_ref[...].astype(jnp.float32) * (1.0 / GRID)
    amp = amp_ref[...]
    aber = aber_ref[...]
    amp_cos = jnp.transpose(amp * jnp.cos(aber))
    amp_sin = jnp.transpose(amp * jnp.sin(aber))
    pl.semaphore_wait(barrier, 3)

    def ring(buf, ss, rs, way, dist):
        src = (-way * (dist - 1)) % peers
        dst = (-way * dist) % peers
        return pltpu.make_async_remote_copy(
            src_ref=buf.at[src], dst_ref=buf.at[dst], send_sem=ss.at[dst], recv_sem=rs.at[dst],
            device_id={"probe": at_offset(way)}, device_id_type=MESH,
        )

    def moves(dist):
        if dist == 0 or dist > peers // 2:
            return []
        ways = (1, -1) if 2 * dist < peers else (1,)
        return [
            ring(buf, ss, rs, way, dist)
            for buf, ss, rs in ((posbuf, pos_ss, pos_rs), (patbuf, pat_ss, pat_rs))
            for way in ways
        ]

    started = []
    passed = [0]

    def forward():
        for copy in moves(passed[0]):
            copy.wait_recv()
        for copy in moves(passed[0] + 1):
            copy.start()
            started.append(copy)
        passed[0] += 1

    forward()

    for g in range(groups):
        if g * LANES % piece == 0:
            s_copies[g * LANES // piece].wait()
        s_blk = s_v[g * LANES : (g + 1) * LANES, :].astype(jnp.float32)
        s_re, s_im = s_blk[:, :pix], s_blk[:, pix:]
        fc, fs = amp_cos[:, g : g + 1], amp_sin[:, g : g + 1]
        c_re = fc * s_re + fs * s_im
        c_im = fc * s_im - fs * s_re
        base = 2 * g * LANES
        w_v[base : base + LANES, :pix] = c_re.astype(jnp.bfloat16)
        w_v[base : base + LANES, pix:] = c_im.astype(jnp.bfloat16)
        w_v[base + LANES : base + 2 * LANES, :pix] = c_im.astype(jnp.bfloat16)
        w_v[base + LANES : base + 2 * LANES, pix:] = (-c_re).astype(jnp.bfloat16)

    def columns(first, end):
        def group(g, carry):
            cols = pl.ds(pl.multiple_of(g * LANES, LANES), LANES)
            k1, k2 = kf[0:1, cols], kf[1:2, cols]
            wrows = pl.ds(pl.multiple_of(g * 2 * LANES, 2 * LANES), 2 * LANES)
            pltpu.matmul_push_rhs(w_v[wrows, :pix], 0, 0)
            pltpu.matmul_push_rhs(w_v[wrows, pix:], 0, 1)
            for n in range(2):
                prow = pl.ds(n * pair_rows, pair_rows)
                cos_t, sin_t = cos_sin_turns(pb[0, prow, :] * k1 + pb[1, prow, :] * k2)
                lhs = jnp.concatenate(
                    [cos_t.astype(jnp.bfloat16), sin_t.astype(jnp.bfloat16)], axis=1
                )
                staged = 0 if n == 0 else None
                pltpu.matmul_acc_lhs(left[n], lhs, load_staged_rhs=staged)
                pltpu.matmul_acc_lhs(right[n], lhs, load_staged_rhs=staged)
            return carry

        lax.fori_loop(first, end, group, 0, unroll=2)

    def psi_copy(i):
        return pltpu.make_async_remote_copy(
            src_ref=psend.at[i], dst_ref=precv.at[i], send_sem=psi_ss.at[i], recv_sem=psi_rs.at[i],
            device_id={"beam": 1 - core}, device_id_type=MESH,
        )

    def waves(i, offsets):
        while passed[0] <= max(min(o, peers - o) for o in offsets):
            forward()
        for n, owner in enumerate((1 - core, core)):
            for j, offset in enumerate(offsets):
                for t in range(part // LANES):
                    for axis in range(2):
                        lo = pl.multiple_of(owner * part + t * LANES, LANES)
                        line = posbuf[offset, axis : axis + 1, pl.ds(lo, LANES)]
                        row = n * pair_rows + j * part + t * LANES
                        pb[axis, row : row + LANES, :] = jnp.transpose(
                            jnp.broadcast_to(line.astype(jnp.float32), (LANES, LANES))
                        )
        middle = groups // 2
        columns(0, middle)
        if passed[0] <= peers // 2:
            forward()
        columns(middle, groups)
        psend[i, :, :pix] = pltpu.matmul_pop(left[0])
        psend[i, :, pix:] = pltpu.matmul_pop(right[0])
        copy = psi_copy(i)
        copy.start()
        started.append(copy)
        pown[i, :, :pix] = pltpu.matmul_pop(left[1])
        pown[i, :, pix:] = pltpu.matmul_pop(right[1])

    def quadratic():
        while passed[0] <= peers // 2:
            forward()
        g_copy.wait()
        per = patbuf.shape[1] // 2
        p_all = patbuf[...].astype(jnp.float32)
        p_re = jnp.concatenate([p_all[d, :per] for d in range(peers)], axis=0)
        p_im = jnp.concatenate([p_all[d, per:] for d in range(peers)], axis=0)
        mine = jnp.concatenate(
            [jnp.where(col_ref[at_offset(d)] == me, 1.0, 0.0) for d in range(peers)], axis=1
        )
        lhs = jnp.concatenate([jnp.transpose(p_re) * mine, jnp.transpose(p_im) * mine], axis=1)
        rhs = jnp.concatenate(
            [jnp.concatenate([p_re, -p_im], axis=1), jnp.concatenate([p_im, p_re], axis=1)], axis=0
        )
        spare = -lhs.shape[1] % pix
        if spare:
            lhs = jnp.concatenate([lhs, jnp.zeros((pix, spare), jnp.float32)], axis=1)
            rhs = jnp.concatenate([rhs, jnp.zeros((spare, width), jnp.float32)], axis=0)
        lhs, rhs = lhs.astype(jnp.bfloat16), rhs.astype(jnp.bfloat16)
        for lo in range(0, lhs.shape[1], pix):
            pltpu.matmul_push_rhs(rhs[lo : lo + pix, :pix], 0, 0)
            pltpu.matmul_push_rhs(rhs[lo : lo + pix, pix:], 0, 1)
            pltpu.matmul_acc_lhs(left_end, lhs[:, lo : lo + pix], load_staged_rhs=0)
            pltpu.matmul_acc_lhs(right_end, lhs[:, lo : lo + pix], load_staged_rhs=0)
        q_re, q_im = pltpu.matmul_pop(left_end), pltpu.matmul_pop(right_end)
        g_re, g_im = g_v[0], g_v[1]
        scale = 1.0 / float(pix * (pix // 2))
        m_re = (q_re * g_re - q_im * g_im) * scale
        m_im = (q_re * g_im + q_im * g_re) * (2.0 * scale)
        for lo, m in ((0, m_re), (pix, m_im)):
            high = m.astype(jnp.bfloat16)
            nmat[0, :, lo : lo + pix] = high
            nmat[1, :, lo : lo + pix] = (m - high.astype(jnp.float32)).astype(jnp.bfloat16)

    def result(offset, send):
        idx = at_offset(offset if send else -offset)
        return pltpu.make_async_remote_copy(
            src_ref=osend.at[offset], dst_ref=orecv.at[me if send else idx],
            send_sem=out_ss.at[offset], recv_sem=out_rs.at[me if send else idx],
            device_id={"probe": at_offset(offset)}, device_id_type=MESH,
        )

    def finish(i, offsets):
        psi_copy(i).wait_recv()
        psi = (pown[i] + precv[i]).astype(jnp.bfloat16)
        a, b = psi[:, :pix], psi[:, pix:]
        for term in range(2):
            pltpu.matmul_push_rhs(nmat[term, :, :pix], 0, 0)
            pltpu.matmul_push_rhs(nmat[term, :, pix:], 0, 1)
            pltpu.matmul_acc_lhs(left_end, a, load_staged_rhs=0)
            pltpu.matmul_acc_lhs(right_end, a, load_staged_rhs=0)
            pltpu.matmul_push_rhs(nmat[term, :, :pix], 0, 1)
            pltpu.matmul_acc_lhs(right_end, b, load_staged_rhs=0)
        z = pltpu.matmul_pop(left_end) * a.astype(jnp.float32)
        z += pltpu.matmul_pop(right_end) * b.astype(jnp.float32)
        z = z[:, :LANES] + z[:, LANES:]
        for j, offset in enumerate(offsets):
            for t in range(0, part, LANES):
                row = j * part + t
                turned = jnp.transpose(z[row : row + LANES, :])
                total = turned[0:8]
                for lo in range(8, LANES, 8):
                    total += turned[lo : lo + 8]
                osend[offset, :, t : t + LANES] = total
            if offset:
                copy = result(offset, True)
                copy.start()
                started.append(copy)

    todo = chunk_order(peers)
    for i, offsets in enumerate(todo):
        waves(i, offsets)
        if i == 1:
            quadratic()
        if i >= 1:
            finish(i - 1, todo[i - 1])
    finish(chunks - 1, todo[-1])
    orecv[me] = osend[0]
    for offset in range(1, peers):
        result(offset, False).wait_recv()
    out_ref[...] = jnp.sum(orecv[...], axis=1)
    for copy in started:
        copy.wait_send()


def scoped_kernel(peers, pair_rows, *refs):
    pix = refs[0].shape[1] // 2
    acc = [pltpu.ACC(mxu)((pair_rows, pix), jnp.float32) for mxu in (0, 0, 1, 1)]
    end = [pltpu.ACC(mxu)((max(pair_rows, pix), pix), jnp.float32) for mxu in (0, 1)]
    pl.run_scoped(functools.partial(kernel, peers, *refs), *acc, *end)


def shards(smatrix, aperture, aberration, beam_k, probe_pos, patches, patch_col):
    peers = lax.axis_size("probe")
    beams, _, width = smatrix.shape
    here = probe_pos.shape[1]
    part = here // lax.axis_size("beam")
    per = patches.shape[0]
    pix = width // 2
    chunks = peers // 2
    overlap = overlap_table(PSIDE)
    vmem = pl.BlockSpec(memory_space=pltpu.VMEM)
    hbm = pl.BlockSpec(memory_space=pl.ANY)
    f32, bf16 = jnp.float32, jnp.bfloat16
    waves = pltpu.VMEM((chunks, 2 * part, width), f32)
    results = pltpu.VMEM((peers, 8, part), f32)
    slots = pltpu.SemaphoreType.DMA((peers,))
    each = pltpu.SemaphoreType.DMA((chunks,))
    return pl.pallas_call(
        functools.partial(scoped_kernel, peers, 2 * part),
        out_shape=jax.ShapeDtypeStruct((peers, part), f32),
        in_specs=[hbm, vmem, vmem, vmem, vmem, vmem, vmem, hbm],
        out_specs=vmem,
        scratch_shapes=[
            pltpu.VMEM((beams, width), bf16),
            pltpu.VMEM((2 * beams, width), bf16),
            pltpu.VMEM(overlap.shape, f32),
            pltpu.VMEM((2, beams), f32),
            pltpu.VMEM((2, 4 * part, LANES), f32),
            pltpu.VMEM((peers, 2, here), jnp.int32),
            pltpu.VMEM((peers, 2 * per, pix), bf16),
            pltpu.VMEM((2, pix, width), bf16),
            waves, waves, waves, results, results,
            pltpu.SemaphoreType.DMA((4,)), pltpu.SemaphoreType.DMA((1,)),
            slots, slots, slots, slots, each, each, slots, slots,
        ],
        compiler_params=pltpu.CompilerParams(
            collective_id=0, has_side_effects=True, vmem_limit_bytes=56 << 20
        ),
    )(
        smatrix.reshape(beams, width),
        aperture.reshape(beams // LANES, LANES),
        aberration.reshape(beams // LANES, LANES),
        beam_k,
        probe_pos,
        patches,
        patch_col.reshape(peers, 1, per),
        jnp.asarray(overlap),
    )


def solution(mesh):
    placed = (
        P(("grp", "beam"), "probe", None),
        P("beam"),
        P("beam"),
        P(None, "beam"),
        P(None, "probe"),
        P(("grp", "probe"), None),
        P("grp"),
    )
    whole = jax.shard_map(
        shards, mesh=mesh, in_specs=placed, out_specs=P("grp", ("probe", "beam")), check_vma=False
    )

    def run(*args):
        with jax.sharding.use_abstract_mesh(mesh.abstract_mesh):
            return whole(*args)

    return run
```

```python
import functools
import math

import jax
import jax.numpy as jnp
import numpy as np
from jax import lax
from jax.experimental import pallas as pl
from jax.experimental.pallas import tpu as pltpu
from jax.sharding import PartitionSpec as P

PSIDE = 16
GRID = 1024
LANES = 128
ROUND = 1.5 * 2.0**23
MESH = pl.DeviceIdType.MESH


def overlap_table(edge_count):
    half_side = edge_count // 2
    pixel = np.arange(edge_count * edge_count)
    mode = np.arange(edge_count * half_side)
    first = mode // half_side - half_side
    second = mode % half_side - edge_count // 4
    turns = np.mod(
        (pixel // edge_count)[:, None] * first[None, :]
        + (pixel % edge_count)[:, None] * second[None, :],
        edge_count,
    )
    angle = np.float32(2.0 * math.pi / edge_count) * turns.astype(np.float32)
    e_re = np.cos(angle).astype(jnp.bfloat16).astype(np.float64)
    e_im = (-np.sin(angle)).astype(jnp.bfloat16).astype(np.float64)
    g_re = e_re @ e_re.T + e_im @ e_im.T
    g_im = e_im @ e_re.T - e_re @ e_im.T
    return np.stack([g_re, g_im]).astype(np.float32)


def cos_sin_turns(u):
    r = u - ((u + ROUND) - ROUND)
    x = r * r
    s = r * (4.4415360 + x * (-7.2646804 + x * 3.2520479))
    c = 1.4142041 + x * (-6.9776420 + x * (5.7152380 + x * -1.7283475))
    return 1.0 - s * s, s * c


def ring_spot(index, peers):
    if peers != 8:
        return index
    line, along = lax.rem(index, 2), index // 2
    return along * (1 - line) + (peers - 1 - along) * line


def ring_index(spot, peers):
    if peers != 8:
        return spot
    line = spot // (peers // 2)
    return 2 * spot * (1 - line) + (2 * (peers - 1 - spot) + 1) * line


def chunk_order(peers):
    far = [d for d in range(3, peers - 1) if d not in (peers // 2, peers - 2)] + [peers // 2, 2]
    far = far + [peers - 2, 1]
    return [(0,)] + [tuple(far[i : i + 2]) for i in range(0, len(far), 2)] + [(peers - 1,)]


def kernel(
    peers, s_hbm, amp_ref, aber_ref, k_ref, pos_ref, pat_ref, col_ref, g_hbm, out_ref,
    s_v, w_v, g_v, kf, pb, posbuf, patbuf, nmat, psend, pown, precv, osend, orecv,
    s_sem, g_sem, pos_ss, pos_rs, pat_ss, pat_rs, psi_ss, psi_rs, out_ss, out_rs,
    *accs,
):
    me = lax.axis_index("probe")
    core = lax.axis_index("beam")
    beams, width = s_v.shape
    pix = width // 2
    groups = beams // LANES
    part = pos_ref.shape[1] // 2
    todo = chunk_order(peers)
    ends = accs[:2]
    pairs, singles = accs[2:6], accs[6:10]

    spot = ring_spot(me, peers)

    def at_offset(offset):
        return ring_index(lax.rem(spot + offset + peers, peers), peers)

    pieces = s_sem.shape[0]
    piece = beams // pieces
    s_copies = [
        pltpu.make_async_copy(
            s_hbm.at[pl.ds(i * piece, piece)], s_v.at[pl.ds(i * piece, piece)], s_sem.at[i]
        )
        for i in range(pieces)
    ]
    for copy in s_copies:
        copy.start()
    g_copy = pltpu.make_async_copy(g_hbm, g_v, g_sem.at[0])
    g_copy.start()

    barrier = pltpu.get_barrier_semaphore()
    for offset in range(1, peers):
        pl.semaphore_signal(
            barrier, inc=1, device_id={"probe": at_offset(offset)}, device_id_type=MESH
        )
    pl.semaphore_signal(barrier, inc=1, device_id={"beam": 1 - core}, device_id_type=MESH)

    posbuf[0] = pos_ref[...]
    pat = pat_ref[...].astype(jnp.float32)
    patbuf[me] = jnp.concatenate([pat[:, :pix], pat[:, pix:]], axis=0).astype(jnp.bfloat16)
    kf[...] = k_ref[...].astype(jnp.float32) * (1.0 / GRID)
    amp = amp_ref[...]
    aber = aber_ref[...]
    amp_cos = jnp.transpose(amp * jnp.cos(aber))
    amp_sin = jnp.transpose(amp * jnp.sin(aber))

    def position(offset, send):
        slot = peers - offset if send else offset
        return pltpu.make_async_remote_copy(
            src_ref=posbuf.at[0], dst_ref=posbuf.at[slot], send_sem=pos_ss.at[offset],
            recv_sem=pos_rs.at[slot], device_id={"probe": at_offset(offset)}, device_id_type=MESH,
        )

    def patch(offset, send):
        idx = me if send else at_offset(offset)
        return pltpu.make_async_remote_copy(
            src_ref=patbuf.at[idx], dst_ref=patbuf.at[idx], send_sem=pat_ss.at[offset],
            recv_sem=pat_rs.at[idx], device_id={"probe": at_offset(offset)}, device_id_type=MESH,
        )

    started = []

    def hand_out():
        pl.semaphore_wait(barrier, peers)
        receivers = [peers - o for offsets in todo for o in offsets if o]
        for move in (position, patch):
            for offset in receivers:
                copy = move(offset, True)
                copy.start()
                started.append(copy)

    for g in range(groups):
        if g * LANES % piece == 0:
            s_copies[g * LANES // piece].wait()
        s_blk = s_v[g * LANES : (g + 1) * LANES, :].astype(jnp.float32)
        s_re, s_im = s_blk[:, :pix], s_blk[:, pix:]
        fc, fs = amp_cos[:, g : g + 1], amp_sin[:, g : g + 1]
        c_re = fc * s_re + fs * s_im
        c_im = fc * s_im - fs * s_re
        base = 2 * g * LANES
        w_v[base : base + LANES, :pix] = c_re.astype(jnp.bfloat16)
        w_v[base : base + LANES, pix:] = c_im.astype(jnp.bfloat16)
        w_v[base + LANES : base + 2 * LANES, :pix] = c_im.astype(jnp.bfloat16)
        w_v[base + LANES : base + 2 * LANES, pix:] = (-c_re).astype(jnp.bfloat16)
        if g == groups // pieces - 1:
            hand_out()

    def accumulators(offsets):
        left, right = (pairs[:2], pairs[2:]) if len(offsets) == 2 else (singles[:2], singles[2:])
        return left, right, len(offsets) * part

    def columns(offsets):
        left, right, height = accumulators(offsets)

        def group(g, carry):
            cols = pl.ds(pl.multiple_of(g * LANES, LANES), LANES)
            k1, k2 = kf[0:1, cols], kf[1:2, cols]
            wrows = pl.ds(pl.multiple_of(g * 2 * LANES, 2 * LANES), 2 * LANES)
            pltpu.matmul_push_rhs(w_v[wrows, :pix], 0, 0)
            pltpu.matmul_push_rhs(w_v[wrows, pix:], 0, 1)
            for n in range(2):
                prow = pl.ds(n * height, height)
                cos_t, sin_t = cos_sin_turns(pb[0, prow, :] * k1 + pb[1, prow, :] * k2)
                lhs = jnp.concatenate(
                    [cos_t.astype(jnp.bfloat16), sin_t.astype(jnp.bfloat16)], axis=1
                )
                staged = 0 if n == 0 else None
                pltpu.matmul_acc_lhs(left[n], lhs, load_staged_rhs=staged)
                pltpu.matmul_acc_lhs(right[n], lhs, load_staged_rhs=staged)
            return carry

        lax.fori_loop(0, groups, group, 0, unroll=2)

    def psi_copy(i):
        span = pl.ds(0, len(todo[i]) * part)
        return pltpu.make_async_remote_copy(
            src_ref=psend.at[i, span], dst_ref=precv.at[i, span], send_sem=psi_ss.at[i],
            recv_sem=psi_rs.at[i], device_id={"beam": 1 - core}, device_id_type=MESH,
        )

    def waves(i):
        offsets = todo[i]
        left, right, height = accumulators(offsets)
        for j, offset in enumerate(offsets):
            if offset:
                position(offset, False).wait_recv()
            for n, owner in enumerate((1 - core, core)):
                for t in range(part // LANES):
                    for axis in range(2):
                        lo = pl.multiple_of(owner * part + t * LANES, LANES)
                        line = posbuf[offset, axis : axis + 1, pl.ds(lo, LANES)]
                        row = n * height + j * part + t * LANES
                        pb[axis, row : row + LANES, :] = jnp.transpose(
                            jnp.broadcast_to(line.astype(jnp.float32), (LANES, LANES))
                        )
        columns(offsets)
        psend[i, :height, :pix] = pltpu.matmul_pop(left[0])
        psend[i, :height, pix:] = pltpu.matmul_pop(right[0])
        copy = psi_copy(i)
        copy.start()
        started.append(copy)
        pown[i, :height, :pix] = pltpu.matmul_pop(left[1])
        pown[i, :height, pix:] = pltpu.matmul_pop(right[1])

    def quadratic():
        for offset in range(1, peers):
            patch(offset, False).wait_recv()
        g_copy.wait()
        per = patbuf.shape[1] // 2
        p_all = patbuf[...].astype(jnp.float32)
        p_re = jnp.concatenate([p_all[d, :per] for d in range(peers)], axis=0)
        p_im = jnp.concatenate([p_all[d, per:] for d in range(peers)], axis=0)
        mine = jnp.where(col_ref[...] == me, 1.0, 0.0)
        lhs = jnp.concatenate([jnp.transpose(p_re) * mine, jnp.transpose(p_im) * mine], axis=1)
        rhs = jnp.concatenate(
            [jnp.concatenate([p_re, -p_im], axis=1), jnp.concatenate([p_im, p_re], axis=1)], axis=0
        )
        spare = -lhs.shape[1] % pix
        if spare:
            lhs = jnp.concatenate([lhs, jnp.zeros((pix, spare), jnp.float32)], axis=1)
            rhs = jnp.concatenate([rhs, jnp.zeros((spare, width), jnp.float32)], axis=0)
        lhs, rhs = lhs.astype(jnp.bfloat16), rhs.astype(jnp.bfloat16)
        for lo in range(0, lhs.shape[1], pix):
            pltpu.matmul_push_rhs(rhs[lo : lo + pix, :pix], 0, 0)
            pltpu.matmul_push_rhs(rhs[lo : lo + pix, pix:], 0, 1)
            pltpu.matmul_acc_lhs(ends[0], lhs[:, lo : lo + pix], load_staged_rhs=0)
            pltpu.matmul_acc_lhs(ends[1], lhs[:, lo : lo + pix], load_staged_rhs=0)
        q_re, q_im = pltpu.matmul_pop(ends[0]), pltpu.matmul_pop(ends[1])
        g_re, g_im = g_v[0], g_v[1]
        scale = 1.0 / float(pix * (pix // 2))
        m_re = (q_re * g_re - q_im * g_im) * scale
        m_im = (q_re * g_im + q_im * g_re) * (2.0 * scale)
        for lo, m in ((0, m_re), (pix, m_im)):
            high = m.astype(jnp.bfloat16)
            nmat[0, :, lo : lo + pix] = high
            nmat[1, :, lo : lo + pix] = (m - high.astype(jnp.float32)).astype(jnp.bfloat16)

    def result(offset, send):
        idx = at_offset(offset if send else -offset)
        return pltpu.make_async_remote_copy(
            src_ref=osend.at[offset], dst_ref=orecv.at[me if send else idx],
            send_sem=out_ss.at[offset], recv_sem=out_rs.at[me if send else idx],
            device_id={"probe": at_offset(offset)}, device_id_type=MESH,
        )

    def finish(i):
        offsets = todo[i]
        height = len(offsets) * part
        left, right = ends if len(offsets) == 2 else (singles[0], singles[2])
        psi_copy(i).wait_recv()
        psi = (pown[i, :height] + precv[i, :height]).astype(jnp.bfloat16)
        a, b = psi[:, :pix], psi[:, pix:]
        for term in range(2):
            pltpu.matmul_push_rhs(nmat[term, :, :pix], 0, 0)
            pltpu.matmul_push_rhs(nmat[term, :, pix:], 0, 1)
            pltpu.matmul_acc_lhs(left, a, load_staged_rhs=0)
            pltpu.matmul_acc_lhs(right, a, load_staged_rhs=0)
            pltpu.matmul_push_rhs(nmat[term, :, :pix], 0, 1)
            pltpu.matmul_acc_lhs(right, b, load_staged_rhs=0)
        z = pltpu.matmul_pop(left) * a.astype(jnp.float32)
        z += pltpu.matmul_pop(right) * b.astype(jnp.float32)
        z = z[:, :LANES] + z[:, LANES:]
        for j, offset in enumerate(offsets):
            for t in range(0, part, LANES):
                row = j * part + t
                turned = jnp.transpose(z[row : row + LANES, :])
                total = turned[0:8]
                for lo in range(8, LANES, 8):
                    total += turned[lo : lo + 8]
                osend[offset, :, t : t + LANES] = total
            if offset:
                copy = result(offset, True)
                copy.start()
                started.append(copy)

    for i in range(len(todo)):
        waves(i)
        if i == 1:
            quadratic()
        if i >= 1:
            finish(i - 1)
    finish(len(todo) - 1)
    orecv[me] = osend[0]
    for offset in range(1, peers):
        result(offset, False).wait_recv()
    out_ref[...] = jnp.sum(orecv[...], axis=1)
    for copy in started:
        copy.wait_send()


def scoped_kernel(peers, part, *refs):
    pix = refs[0].shape[1] // 2
    accs = [pltpu.ACC(mxu)((pix, pix), jnp.float32) for mxu in (0, 1)]
    for rows in (2 * part, part):
        accs += [pltpu.ACC(mxu)((rows, pix), jnp.float32) for mxu in (0, 0, 1, 1)]
    pl.run_scoped(functools.partial(kernel, peers, *refs), *accs)


def shards(smatrix, aperture, aberration, beam_k, probe_pos, patches, patch_col):
    peers = lax.axis_size("probe")
    beams, _, width = smatrix.shape
    here = probe_pos.shape[1]
    part = here // lax.axis_size("beam")
    per = patches.shape[0]
    pix = width // 2
    chunks = len(chunk_order(peers))
    overlap = overlap_table(PSIDE)
    vmem = pl.BlockSpec(memory_space=pltpu.VMEM)
    hbm = pl.BlockSpec(memory_space=pl.ANY)
    f32, bf16 = jnp.float32, jnp.bfloat16
    waves = pltpu.VMEM((chunks, 2 * part, width), f32)
    results = pltpu.VMEM((peers, 8, part), f32)
    slots = pltpu.SemaphoreType.DMA((peers,))
    each = pltpu.SemaphoreType.DMA((chunks,))
    return pl.pallas_call(
        functools.partial(scoped_kernel, peers, part),
        out_shape=jax.ShapeDtypeStruct((peers, part), f32),
        in_specs=[hbm, vmem, vmem, vmem, vmem, vmem, vmem, hbm],
        out_specs=vmem,
        scratch_shapes=[
            pltpu.VMEM((beams, width), bf16),
            pltpu.VMEM((2 * beams, width), bf16),
            pltpu.VMEM(overlap.shape, f32),
            pltpu.VMEM((2, beams), f32),
            pltpu.VMEM((2, 4 * part, LANES), f32),
            pltpu.VMEM((peers, 2, here), jnp.int32),
            pltpu.VMEM((peers, 2 * per, pix), bf16),
            pltpu.VMEM((2, pix, width), bf16),
            waves, waves, waves, results, results,
            pltpu.SemaphoreType.DMA((4,)), pltpu.SemaphoreType.DMA((1,)),
            slots, slots, slots, slots, each, each, slots, slots,
        ],
        compiler_params=pltpu.CompilerParams(
            collective_id=0, has_side_effects=True, vmem_limit_bytes=56 << 20
        ),
    )(
        smatrix.reshape(beams, width),
        aperture.reshape(beams // LANES, LANES),
        aberration.reshape(beams // LANES, LANES),
        beam_k,
        probe_pos,
        patches,
        patch_col.reshape(1, patch_col.shape[0]),
        jnp.asarray(overlap),
    )


def solution(mesh):
    placed = (
        P(("grp", "beam"), "probe", None),
        P("beam"),
        P("beam"),
        P(None, "beam"),
        P(None, "probe"),
        P(("grp", "probe"), None),
        P("grp"),
    )
    whole = jax.shard_map(
        shards, mesh=mesh, in_specs=placed, out_specs=P("grp", ("probe", "beam")), check_vma=False
    )

    def run(*args):
        with jax.sharding.use_abstract_mesh(mesh.abstract_mesh):
            return whole(*args)

    return run
```

```python
import functools
import math

import jax
import jax.numpy as jnp
import numpy as np
from jax import lax
from jax.experimental import pallas as pl
from jax.experimental.pallas import tpu as pltpu
from jax.sharding import PartitionSpec as P

PSIDE = 16
GRID = 1024
LANES = 128
ROUND = 1.5 * 2.0**23
MESH = pl.DeviceIdType.MESH


def overlap_table(edge_count):
    half_side = edge_count // 2
    pixel = np.arange(edge_count * edge_count)
    mode = np.arange(edge_count * half_side)
    first = mode // half_side - half_side
    second = mode % half_side - edge_count // 4
    turns = np.mod(
        (pixel // edge_count)[:, None] * first[None, :]
        + (pixel % edge_count)[:, None] * second[None, :],
        edge_count,
    )
    angle = np.float32(2.0 * math.pi / edge_count) * turns.astype(np.float32)
    e_re = np.cos(angle).astype(jnp.bfloat16).astype(np.float64)
    e_im = (-np.sin(angle)).astype(jnp.bfloat16).astype(np.float64)
    g_re = e_re @ e_re.T + e_im @ e_im.T
    g_im = e_im @ e_re.T - e_re @ e_im.T
    return np.stack([g_re, g_im]).astype(np.float32)


def fraction(u):
    return u - ((u + ROUND) - ROUND)


def cos_sin_turns(u):
    r = fraction(u)
    x = r * r
    s = r * (4.4428679 + x * (-7.3074434 + x * (3.5947879 + x * -0.7843736)))
    c = 1.4142041 + x * (-6.9776420 + x * (5.7152380 + x * -1.7283475))
    return 1.0 - s * s, s * c


COS_UNIT = 10.575109
SIN_UNIT = 16.216523


def scaled_cos_sin_turns(u):
    r = fraction(u)
    x = r * r
    s = r * ((x - 2.2338787) * x + 1.3657659)
    c = (x - 1.3820002) * x + 0.28310711
    return 0.094555356 - s * s, s * c


def ring_spot(index, peers):
    if peers != 8:
        return index
    line, along = lax.rem(index, 2), index // 2
    return along * (1 - line) + (peers - 1 - along) * line


def ring_index(spot, peers):
    if peers != 8:
        return spot
    line = spot // (peers // 2)
    return 2 * spot * (1 - line) + (2 * (peers - 1 - spot) + 1) * line


def chunk_order(peers):
    far = [d for d in range(3, peers - 1) if d not in (peers // 2, peers - 2)] + [peers // 2, 2]
    far = far + [peers - 2, 1]
    return [(0,)] + [tuple(far[i : i + 2]) for i in range(0, len(far), 2)] + [(peers - 1,)]


def kernel(
    peers, s_hbm, amp_ref, aber_ref, k_ref, pos_ref, pat_ref, col_ref, g_hbm, out_ref,
    s_v, w_v, g_v, kf, pb, posbuf, patbuf, nmat, psend, pown, precv, osend, orecv,
    s_sem, g_sem, pos_ss, pos_rs, pat_ss, pat_rs, psi_ss, psi_rs, out_ss, out_rs,
    *accs,
):
    me = lax.axis_index("probe")
    core = lax.axis_index("beam")
    beams, width = s_v.shape
    pix = width // 2
    groups = beams // LANES
    part = pos_ref.shape[1] // 2
    todo = chunk_order(peers)
    ends = accs[:2]
    pairs, singles = accs[2:6], accs[6:10]

    spot = ring_spot(me, peers)

    def at_offset(offset):
        return ring_index(lax.rem(spot + offset + peers, peers), peers)

    pieces = s_sem.shape[0]
    piece = beams // pieces
    s_copies = [
        pltpu.make_async_copy(
            s_hbm.at[pl.ds(i * piece, piece)], s_v.at[pl.ds(i * piece, piece)], s_sem.at[i]
        )
        for i in range(pieces)
    ]
    for copy in s_copies:
        copy.start()
    g_copy = pltpu.make_async_copy(g_hbm, g_v, g_sem.at[0])
    g_copy.start()

    barrier = pltpu.get_barrier_semaphore()
    for offset in range(1, peers):
        pl.semaphore_signal(
            barrier, inc=1, device_id={"probe": at_offset(offset)}, device_id_type=MESH
        )
    pl.semaphore_signal(barrier, inc=1, device_id={"beam": 1 - core}, device_id_type=MESH)

    posbuf[0] = pos_ref[...]
    pat = pat_ref[...].astype(jnp.float32)
    patbuf[me] = jnp.concatenate([pat[:, :pix], pat[:, pix:]], axis=0).astype(jnp.bfloat16)
    kf[...] = k_ref[...].astype(jnp.float32) * (1.0 / GRID)
    amp = amp_ref[...]
    aber = aber_ref[...]
    aber_cos, aber_sin = cos_sin_turns(aber * (0.5 / math.pi))
    amp_cos = jnp.transpose(amp * aber_cos)
    amp_sin = jnp.transpose(amp * aber_sin)

    def position(offset, send):
        slot = peers - offset if send else offset
        return pltpu.make_async_remote_copy(
            src_ref=posbuf.at[0], dst_ref=posbuf.at[slot], send_sem=pos_ss.at[offset],
            recv_sem=pos_rs.at[slot], device_id={"probe": at_offset(offset)}, device_id_type=MESH,
        )

    def patch(offset, send):
        idx = me if send else at_offset(offset)
        return pltpu.make_async_remote_copy(
            src_ref=patbuf.at[idx], dst_ref=patbuf.at[idx], send_sem=pat_ss.at[offset],
            recv_sem=pat_rs.at[idx], device_id={"probe": at_offset(offset)}, device_id_type=MESH,
        )

    started = []

    def hand_out():
        pl.semaphore_wait(barrier, peers)
        receivers = [peers - o for offsets in todo for o in offsets if o]
        for move in (position, patch):
            for offset in receivers:
                copy = move(offset, True)
                copy.start()
                started.append(copy)

    for g in range(groups):
        if g * LANES % piece == 0:
            s_copies[g * LANES // piece].wait()
        s_blk = s_v[g * LANES : (g + 1) * LANES, :].astype(jnp.float32)
        s_re, s_im = s_blk[:, :pix], s_blk[:, pix:]
        fc, fs = amp_cos[:, g : g + 1], amp_sin[:, g : g + 1]
        c_re = fc * s_re + fs * s_im
        c_im = fc * s_im - fs * s_re
        base = 2 * g * LANES
        w_v[base : base + LANES, :pix] = (COS_UNIT * c_re).astype(jnp.bfloat16)
        w_v[base : base + LANES, pix:] = (COS_UNIT * c_im).astype(jnp.bfloat16)
        w_v[base + LANES : base + 2 * LANES, :pix] = (SIN_UNIT * c_im).astype(jnp.bfloat16)
        w_v[base + LANES : base + 2 * LANES, pix:] = (-SIN_UNIT * c_re).astype(jnp.bfloat16)
        if g == groups // pieces - 1:
            hand_out()

    def accumulators(offsets):
        left, right = (pairs[:2], pairs[2:]) if len(offsets) == 2 else (singles[:2], singles[2:])
        return left, right, len(offsets) * part

    def columns(offsets):
        left, right, height = accumulators(offsets)

        def group(g, carry):
            cols = pl.ds(pl.multiple_of(g * LANES, LANES), LANES)
            k1, k2 = kf[0:1, cols], kf[1:2, cols]
            wrows = pl.ds(pl.multiple_of(g * 2 * LANES, 2 * LANES), 2 * LANES)
            pltpu.matmul_push_rhs(w_v[wrows, :pix], 0, 0)
            pltpu.matmul_push_rhs(w_v[wrows, pix:], 0, 1)
            for n in range(2):
                prow = pl.ds(n * height, height)
                cos_t, sin_t = scaled_cos_sin_turns(pb[0, prow, :] * k1 + pb[1, prow, :] * k2)
                lhs = jnp.concatenate(
                    [cos_t.astype(jnp.bfloat16), sin_t.astype(jnp.bfloat16)], axis=1
                )
                staged = 0 if n == 0 else None
                pltpu.matmul_acc_lhs(left[n], lhs, load_staged_rhs=staged)
                pltpu.matmul_acc_lhs(right[n], lhs, load_staged_rhs=staged)
            return carry

        lax.fori_loop(0, groups, group, 0, unroll=2)

    def psi_copy(i):
        span = pl.ds(0, len(todo[i]) * part)
        return pltpu.make_async_remote_copy(
            src_ref=psend.at[i, span], dst_ref=precv.at[i, span], send_sem=psi_ss.at[i],
            recv_sem=psi_rs.at[i], device_id={"beam": 1 - core}, device_id_type=MESH,
        )

    def waves(i):
        offsets = todo[i]
        left, right, height = accumulators(offsets)
        for j, offset in enumerate(offsets):
            if offset:
                position(offset, False).wait_recv()
            for n, owner in enumerate((1 - core, core)):
                for t in range(part // LANES):
                    for axis in range(2):
                        lo = pl.multiple_of(owner * part + t * LANES, LANES)
                        line = posbuf[offset, axis : axis + 1, pl.ds(lo, LANES)]
                        row = n * height + j * part + t * LANES
                        pb[axis, row : row + LANES, :] = jnp.transpose(
                            jnp.broadcast_to(line.astype(jnp.float32), (LANES, LANES))
                        )
        columns(offsets)
        psend[i, :height, :pix] = pltpu.matmul_pop(left[0])
        psend[i, :height, pix:] = pltpu.matmul_pop(right[0])
        copy = psi_copy(i)
        copy.start()
        started.append(copy)
        pown[i, :height, :pix] = pltpu.matmul_pop(left[1])
        pown[i, :height, pix:] = pltpu.matmul_pop(right[1])

    def quadratic():
        for offset in range(1, peers):
            patch(offset, False).wait_recv()
        g_copy.wait()
        per = patbuf.shape[1] // 2
        p_all = patbuf[...].astype(jnp.float32)
        p_re = jnp.concatenate([p_all[d, :per] for d in range(peers)], axis=0)
        p_im = jnp.concatenate([p_all[d, per:] for d in range(peers)], axis=0)
        mine = jnp.where(col_ref[...] == me, 1.0, 0.0)
        lhs = jnp.concatenate([jnp.transpose(p_re) * mine, jnp.transpose(p_im) * mine], axis=1)
        rhs = jnp.concatenate(
            [jnp.concatenate([p_re, -p_im], axis=1), jnp.concatenate([p_im, p_re], axis=1)], axis=0
        )
        spare = -lhs.shape[1] % pix
        if spare:
            lhs = jnp.concatenate([lhs, jnp.zeros((pix, spare), jnp.float32)], axis=1)
            rhs = jnp.concatenate([rhs, jnp.zeros((spare, width), jnp.float32)], axis=0)
        lhs, rhs = lhs.astype(jnp.bfloat16), rhs.astype(jnp.bfloat16)
        for lo in range(0, lhs.shape[1], pix):
            pltpu.matmul_push_rhs(rhs[lo : lo + pix, :pix], 0, 0)
            pltpu.matmul_push_rhs(rhs[lo : lo + pix, pix:], 0, 1)
            pltpu.matmul_acc_lhs(ends[0], lhs[:, lo : lo + pix], load_staged_rhs=0)
            pltpu.matmul_acc_lhs(ends[1], lhs[:, lo : lo + pix], load_staged_rhs=0)
        q_re, q_im = pltpu.matmul_pop(ends[0]), pltpu.matmul_pop(ends[1])
        g_re, g_im = g_v[0], g_v[1]
        scale = 1.0 / float(pix * (pix // 2))
        m_re = (q_re * g_re - q_im * g_im) * scale
        m_im = (q_re * g_im + q_im * g_re) * (2.0 * scale)
        nmat[:, :pix] = m_re.astype(jnp.bfloat16)
        nmat[:, pix:] = m_im.astype(jnp.bfloat16)

    def result(offset, send):
        idx = at_offset(offset if send else -offset)
        return pltpu.make_async_remote_copy(
            src_ref=osend.at[offset], dst_ref=orecv.at[me if send else idx],
            send_sem=out_ss.at[offset], recv_sem=out_rs.at[me if send else idx],
            device_id={"probe": at_offset(offset)}, device_id_type=MESH,
        )

    def finish(i):
        offsets = todo[i]
        height = len(offsets) * part
        left, right = ends if len(offsets) == 2 else (singles[0], singles[2])
        psi_copy(i).wait_recv()
        psi = (pown[i, :height] + precv[i, :height]).astype(jnp.bfloat16)
        a, b = psi[:, :pix], psi[:, pix:]
        pltpu.matmul_push_rhs(nmat[:, :pix], 0, 0)
        pltpu.matmul_push_rhs(nmat[:, pix:], 0, 1)
        pltpu.matmul_acc_lhs(left, a, load_staged_rhs=0)
        pltpu.matmul_acc_lhs(right, a, load_staged_rhs=0)
        pltpu.matmul_push_rhs(nmat[:, :pix], 0, 1)
        pltpu.matmul_acc_lhs(right, b, load_staged_rhs=0)
        z = pltpu.matmul_pop(left) * a.astype(jnp.float32)
        z += pltpu.matmul_pop(right) * b.astype(jnp.float32)
        z = z[:, :LANES] + z[:, LANES:]
        for j, offset in enumerate(offsets):
            for t in range(0, part, LANES):
                row = j * part + t
                turned = jnp.transpose(z[row : row + LANES, :])
                total = turned[0:8]
                for lo in range(8, LANES, 8):
                    total += turned[lo : lo + 8]
                osend[offset, :, t : t + LANES] = total
            if offset:
                copy = result(offset, True)
                copy.start()
                started.append(copy)

    for i in range(len(todo)):
        waves(i)
        if i == 1:
            quadratic()
        if i >= 1:
            finish(i - 1)
    finish(len(todo) - 1)
    orecv[me] = osend[0]
    for offset in range(1, peers):
        result(offset, False).wait_recv()
    out_ref[...] = jnp.sum(orecv[...], axis=1)
    for copy in started:
        copy.wait_send()


def scoped_kernel(peers, part, *refs):
    pix = refs[0].shape[1] // 2
    accs = [pltpu.ACC(mxu)((pix, pix), jnp.float32) for mxu in (0, 1)]
    for rows in (2 * part, part):
        accs += [pltpu.ACC(mxu)((rows, pix), jnp.float32) for mxu in (0, 0, 1, 1)]
    pl.run_scoped(functools.partial(kernel, peers, *refs), *accs)


def shards(smatrix, aperture, aberration, beam_k, probe_pos, patches, patch_col):
    peers = lax.axis_size("probe")
    beams, _, width = smatrix.shape
    here = probe_pos.shape[1]
    part = here // lax.axis_size("beam")
    per = patches.shape[0]
    pix = width // 2
    chunks = len(chunk_order(peers))
    overlap = overlap_table(PSIDE)
    vmem = pl.BlockSpec(memory_space=pltpu.VMEM)
    hbm = pl.BlockSpec(memory_space=pl.ANY)
    f32, bf16 = jnp.float32, jnp.bfloat16
    waves = pltpu.VMEM((chunks, 2 * part, width), f32)
    results = pltpu.VMEM((peers, 8, part), f32)
    slots = pltpu.SemaphoreType.DMA((peers,))
    each = pltpu.SemaphoreType.DMA((chunks,))
    return pl.pallas_call(
        functools.partial(scoped_kernel, peers, part),
        out_shape=jax.ShapeDtypeStruct((peers, part), f32),
        in_specs=[hbm, vmem, vmem, vmem, vmem, vmem, vmem, hbm],
        out_specs=vmem,
        scratch_shapes=[
            pltpu.VMEM((beams, width), bf16),
            pltpu.VMEM((2 * beams, width), bf16),
            pltpu.VMEM(overlap.shape, f32),
            pltpu.VMEM((2, beams), f32),
            pltpu.VMEM((2, 4 * part, LANES), f32),
            pltpu.VMEM((peers, 2, here), jnp.int32),
            pltpu.VMEM((peers, 2 * per, pix), bf16),
            pltpu.VMEM((pix, width), bf16),
            waves, waves, waves, results, results,
            pltpu.SemaphoreType.DMA((4,)), pltpu.SemaphoreType.DMA((1,)),
            slots, slots, slots, slots, each, each, slots, slots,
        ],
        compiler_params=pltpu.CompilerParams(
            collective_id=0, has_side_effects=True, vmem_limit_bytes=56 << 20
        ),
    )(
        smatrix.reshape(beams, width),
        aperture.reshape(beams // LANES, LANES),
        aberration.reshape(beams // LANES, LANES),
        beam_k,
        probe_pos,
        patches,
        patch_col.reshape(1, patch_col.shape[0]),
        jnp.asarray(overlap),
    )


def solution(mesh):
    placed = (
        P(("grp", "beam"), "probe", None),
        P("beam"),
        P("beam"),
        P(None, "beam"),
        P(None, "probe"),
        P(("grp", "probe"), None),
        P("grp"),
    )
    whole = jax.shard_map(
        shards, mesh=mesh, in_specs=placed, out_specs=P("grp", ("probe", "beam")), check_vma=False
    )

    def run(*args):
        with jax.sharding.use_abstract_mesh(mesh.abstract_mesh):
            return whole(*args)

    return run
```

```python
import functools
import math

import jax
import jax.numpy as jnp
import numpy as np
from jax import lax
from jax.experimental import pallas as pl
from jax.experimental.pallas import tpu as pltpu
from jax.sharding import PartitionSpec as P

PSIDE = 16
GRID = 1024
LANES = 128
ROUND = 1.5 * 2.0**23
MESH = pl.DeviceIdType.MESH


def overlap_table(edge_count):
    half_side = edge_count // 2
    pixel = np.arange(edge_count * edge_count)
    mode = np.arange(edge_count * half_side)
    first = mode // half_side - half_side
    second = mode % half_side - edge_count // 4
    turns = np.mod(
        (pixel // edge_count)[:, None] * first[None, :]
        + (pixel % edge_count)[:, None] * second[None, :],
        edge_count,
    )
    angle = np.float32(2.0 * math.pi / edge_count) * turns.astype(np.float32)
    e_re = np.cos(angle).astype(jnp.bfloat16).astype(np.float64)
    e_im = (-np.sin(angle)).astype(jnp.bfloat16).astype(np.float64)
    g_re = e_re @ e_re.T + e_im @ e_im.T
    g_im = e_im @ e_re.T - e_re @ e_im.T
    return np.stack([g_re, g_im]).astype(np.float32)


def fraction(u):
    return u - ((u + ROUND) - ROUND)


def cos_sin_turns(u):
    r = fraction(u)
    x = r * r
    s = r * (4.4428679 + x * (-7.3074434 + x * (3.5947879 + x * -0.7843736)))
    c = 1.4142041 + x * (-6.9776420 + x * (5.7152380 + x * -1.7283475))
    return 1.0 - s * s, s * c


COS_UNIT = 10.575109
SIN_UNIT = 16.216523


def scaled_cos_sin_turns(u):
    r = fraction(u)
    x = r * r
    s = r * ((x - 2.2338787) * x + 1.3657659)
    c = (x - 1.3820002) * x + 0.28310711
    return 0.094555356 - s * s, s * c


def ring_spot(index, peers):
    if peers != 8:
        return index
    line, along = lax.rem(index, 2), index // 2
    return along * (1 - line) + (peers - 1 - along) * line


def ring_index(spot, peers):
    if peers != 8:
        return spot
    line = spot // (peers // 2)
    return 2 * spot * (1 - line) + (2 * (peers - 1 - spot) + 1) * line


def chunk_order(peers):
    far = [d for d in range(3, peers - 2) if d != peers // 2] + [peers // 2, 2]
    pairs = [tuple(far[i : i + 2]) for i in range(0, len(far), 2)]
    return [(0,)] + pairs + [(peers - 2, 1, peers - 1)]


def kernel(
    peers, s_hbm, amp_hbm, aber_hbm, k_hbm, pos_hbm, pat_hbm, col_hbm, g_hbm, out_ref,
    s_v, w_v, g_v, kf, pb, posbuf, patbuf, nmat, psend, pown, precv, osend, orecv,
    amp_ref, aber_ref, k_ref, col_ref, pat_ref, m_sem, s_sem, g_sem, pos_ss, pos_rs, pat_ss, pat_rs, psi_ss, psi_rs, out_ss, out_rs,
):
    me = lax.axis_index("probe")
    core = lax.axis_index("beam")
    beams, width = s_v.shape
    pix = width // 2
    groups = beams // LANES
    part = posbuf.shape[2] // 2
    todo = chunk_order(peers)

    spot = ring_spot(me, peers)

    def at_offset(offset):
        return ring_index(lax.rem(spot + offset + peers, peers), peers)

    small = (
        (pos_hbm, posbuf.at[0]),
        (pat_hbm, pat_ref),
        (k_hbm, k_ref),
        (amp_hbm, amp_ref),
        (aber_hbm, aber_ref),
        (col_hbm, col_ref),
    )
    small = [pltpu.make_async_copy(x, y, m_sem.at[i]) for i, (x, y) in enumerate(small)]
    for copy in small:
        copy.start()
    pieces = s_sem.shape[0]
    piece = beams // pieces
    s_copies = [
        pltpu.make_async_copy(
            s_hbm.at[pl.ds(i * piece, piece)], s_v.at[pl.ds(i * piece, piece)], s_sem.at[i]
        )
        for i in range(pieces)
    ]
    for copy in s_copies:
        copy.start()
    g_copy = pltpu.make_async_copy(g_hbm, g_v, g_sem.at[0])
    g_copy.start()

    barrier = pltpu.get_barrier_semaphore()
    for offset in range(1, peers):
        pl.semaphore_signal(
            barrier, inc=1, device_id={"probe": at_offset(offset)}, device_id_type=MESH
        )
    pl.semaphore_signal(barrier, inc=1, device_id={"beam": 1 - core}, device_id_type=MESH)

    for copy in small:
        copy.wait()
    pat = pat_ref[...].astype(jnp.float32)
    patbuf[me] = jnp.concatenate([pat[:, :pix], pat[:, pix:]], axis=0).astype(jnp.bfloat16)
    kf[...] = k_ref[...].astype(jnp.float32) * (1.0 / GRID)
    amp = amp_ref[...] * COS_UNIT
    aber = aber_ref[...]
    aber_cos, aber_sin = cos_sin_turns(aber * (0.5 / math.pi))
    amp_cos = jnp.transpose(amp * aber_cos)
    amp_sin = jnp.transpose(amp * aber_sin)

    def position(offset, send):
        slot = peers - offset if send else offset
        return pltpu.make_async_remote_copy(
            src_ref=posbuf.at[0], dst_ref=posbuf.at[slot], send_sem=pos_ss.at[offset],
            recv_sem=pos_rs.at[slot], device_id={"probe": at_offset(offset)}, device_id_type=MESH,
        )

    def patch(offset, send):
        idx = me if send else at_offset(offset)
        return pltpu.make_async_remote_copy(
            src_ref=patbuf.at[idx], dst_ref=patbuf.at[idx], send_sem=pat_ss.at[offset],
            recv_sem=pat_rs.at[idx], device_id={"probe": at_offset(offset)}, device_id_type=MESH,
        )

    started = []

    def hand_out():
        pl.semaphore_wait(barrier, peers)
        receivers = [peers - o for offsets in todo for o in offsets if o]
        for move in (position, patch):
            for offset in receivers:
                copy = move(offset, True)
                copy.start()
                started.append(copy)

    ratio = SIN_UNIT / COS_UNIT
    for g in range(groups):
        if g * LANES % piece == 0:
            s_copies[g * LANES // piece].wait()
        s_blk = s_v[g * LANES : (g + 1) * LANES, :].astype(jnp.float32)
        s_re, s_im = s_blk[:, :pix], s_blk[:, pix:]
        fc, fs = amp_cos[:, g : g + 1], amp_sin[:, g : g + 1]
        c_re = fc * s_re + fs * s_im
        c_im = fc * s_im - fs * s_re
        base = 2 * g * LANES
        w_v[base : base + LANES, :pix] = c_re.astype(jnp.bfloat16)
        w_v[base : base + LANES, pix:] = c_im.astype(jnp.bfloat16)
        w_v[base + LANES : base + 2 * LANES, :pix] = (ratio * c_im).astype(jnp.bfloat16)
        w_v[base + LANES : base + 2 * LANES, pix:] = (-ratio * c_re).astype(jnp.bfloat16)
        if g == groups // pieces - 1:
            hand_out()

    def with_accumulators(body, rows, count):
        shapes = [pltpu.ACC(mxu)((rows, pix), jnp.float32) for mxu in (0, 1) for _ in range(count)]
        pl.run_scoped(lambda *accs: body(accs[:count], accs[count:]), *shapes)

    def columns(left, right, height):
        def group(g, carry):
            cols = pl.ds(pl.multiple_of(g * LANES, LANES), LANES)
            k1, k2 = kf[0:1, cols], kf[1:2, cols]
            wrows = pl.ds(pl.multiple_of(g * 2 * LANES, 2 * LANES), 2 * LANES)
            pltpu.matmul_push_rhs(w_v[wrows, :pix], 0, 0)
            pltpu.matmul_push_rhs(w_v[wrows, pix:], 0, 1)
            for n in range(len(left)):
                prow = pl.ds(n * height, height)
                cos_t, sin_t = scaled_cos_sin_turns(pb[0, prow, :] * k1 + pb[1, prow, :] * k2)
                lhs = jnp.concatenate(
                    [cos_t.astype(jnp.bfloat16), sin_t.astype(jnp.bfloat16)], axis=1
                )
                staged = 0 if n == 0 else None
                pltpu.matmul_acc_lhs(left[n], lhs, load_staged_rhs=staged)
                pltpu.matmul_acc_lhs(right[n], lhs, load_staged_rhs=staged)
            return carry

        lax.fori_loop(0, groups, group, 0, unroll=8)

    def psi_copy(i):
        span = pl.ds(0, len(todo[i]) * part)
        return pltpu.make_async_remote_copy(
            src_ref=psend.at[i, span], dst_ref=precv.at[i, span], send_sem=psi_ss.at[i],
            recv_sem=psi_rs.at[i], device_id={"beam": 1 - core}, device_id_type=MESH,
        )

    def waves(i, sides):
        offsets = todo[i]
        height = len(offsets) * part
        for j, offset in enumerate(offsets):
            if offset and 0 in sides:
                position(offset, False).wait_recv()
            for n, side in enumerate(sides):
                owner = core if side else 1 - core
                for t in range(part // LANES):
                    for axis in range(2):
                        lo = pl.multiple_of(owner * part + t * LANES, LANES)
                        line = posbuf[offset, axis : axis + 1, pl.ds(lo, LANES)]
                        row = n * height + j * part + t * LANES
                        pb[axis, row : row + LANES, :] = jnp.transpose(
                            jnp.broadcast_to(line.astype(jnp.float32), (LANES, LANES))
                        )

        def body(left, right):
            columns(left, right, height)
            for n, side in enumerate(sides):
                dst = pown if side else psend
                dst[i, :height, :pix] = pltpu.matmul_pop(left[n])
                dst[i, :height, pix:] = pltpu.matmul_pop(right[n])
                if not side:
                    copy.start()

        copy = psi_copy(i) if 0 in sides else None
        if copy:
            started.append(copy)
        with_accumulators(body, height, len(sides))

    def quadratic():
        for offset in range(1, peers):
            patch(offset, False).wait_recv()
        g_copy.wait()
        per = patbuf.shape[1] // 2
        p_all = patbuf[...].astype(jnp.float32)
        p_re = jnp.concatenate([p_all[d, :per] for d in range(peers)], axis=0)
        p_im = jnp.concatenate([p_all[d, per:] for d in range(peers)], axis=0)
        mine = jnp.where(col_ref[...] == me, 1.0, 0.0)
        lhs = jnp.concatenate([jnp.transpose(p_re) * mine, jnp.transpose(p_im) * mine], axis=1)
        rhs = jnp.concatenate(
            [jnp.concatenate([p_re, -p_im], axis=1), jnp.concatenate([p_im, p_re], axis=1)], axis=0
        )
        spare = -lhs.shape[1] % pix
        if spare:
            lhs = jnp.concatenate([lhs, jnp.zeros((pix, spare), jnp.float32)], axis=1)
            rhs = jnp.concatenate([rhs, jnp.zeros((spare, width), jnp.float32)], axis=0)
        lhs, rhs = lhs.astype(jnp.bfloat16), rhs.astype(jnp.bfloat16)
        def gram(left, right):
            for lo in range(0, lhs.shape[1], pix):
                pltpu.matmul_push_rhs(rhs[lo : lo + pix, :pix], 0, 0)
                pltpu.matmul_push_rhs(rhs[lo : lo + pix, pix:], 0, 1)
                pltpu.matmul_acc_lhs(left[0], lhs[:, lo : lo + pix], load_staged_rhs=0)
                pltpu.matmul_acc_lhs(right[0], lhs[:, lo : lo + pix], load_staged_rhs=0)
            store_form(pltpu.matmul_pop(left[0]), pltpu.matmul_pop(right[0]))

        with_accumulators(gram, pix, 1)

    def store_form(q_re, q_im):
        g_re, g_im = g_v[0], g_v[1]
        scale = 1.0 / float(pix * (pix // 2))
        m_re = (q_re * g_re - q_im * g_im) * scale
        m_im = (q_re * g_im + q_im * g_re) * (2.0 * scale)
        nmat[:, :pix] = m_re.astype(jnp.bfloat16)
        nmat[:, pix:] = m_im.astype(jnp.bfloat16)

    def result(offset, send):
        idx = at_offset(offset if send else -offset)
        return pltpu.make_async_remote_copy(
            src_ref=osend.at[offset], dst_ref=orecv.at[me if send else idx],
            send_sem=out_ss.at[offset], recv_sem=out_rs.at[me if send else idx],
            device_id={"probe": at_offset(offset)}, device_id_type=MESH,
        )

    def finish(i):
        offsets = todo[i]
        height = len(offsets) * part
        psi_copy(i).wait_recv()
        psi = (pown[i, :height] + precv[i, :height]).astype(jnp.bfloat16)
        a, b = psi[:, :pix], psi[:, pix:]

        def body(left, right):
            pltpu.matmul_push_rhs(nmat[:, :pix], 0, 0)
            pltpu.matmul_push_rhs(nmat[:, pix:], 0, 1)
            pltpu.matmul_acc_lhs(left[0], a, load_staged_rhs=0)
            pltpu.matmul_acc_lhs(right[0], a, load_staged_rhs=0)
            pltpu.matmul_push_rhs(nmat[:, :pix], 0, 1)
            pltpu.matmul_acc_lhs(right[0], b, load_staged_rhs=0)
            z = pltpu.matmul_pop(left[0]) * a.astype(jnp.float32)
            z += pltpu.matmul_pop(right[0]) * b.astype(jnp.float32)
            z = z[:, :LANES] + z[:, LANES:]
            for j, offset in enumerate(offsets):
                for t in range(0, part, LANES):
                    row = j * part + t
                    turned = jnp.transpose(z[row : row + LANES, :])
                    total = turned[0:8]
                    for lo in range(8, LANES, 8):
                        total += turned[lo : lo + 8]
                    osend[offset, :, t : t + LANES] = total
                if offset:
                    copies[j].start()

        copies = [result(offset, True) if offset else None for offset in offsets]
        started.extend(copy for copy in copies if copy)
        with_accumulators(body, height, 1)

    last = len(todo) - 1
    for i in range(last):
        waves(i, (0, 1))
        if i == 1:
            quadratic()
        if i >= 1:
            finish(i - 1)
    waves(last, (0,))
    finish(last - 1)
    waves(last, (1,))
    finish(last)
    orecv[me] = osend[0]
    for offset in range(1, peers):
        result(offset, False).wait_recv()
    out_ref[...] = jnp.sum(orecv[...], axis=1)
    for copy in started:
        copy.wait_send()


def shards(smatrix, aperture, aberration, beam_k, probe_pos, patches, patch_col):
    peers = lax.axis_size("probe")
    beams, _, width = smatrix.shape
    here = probe_pos.shape[1]
    part = here // lax.axis_size("beam")
    per = patches.shape[0]
    pix = width // 2
    chunks = len(chunk_order(peers))
    overlap = overlap_table(PSIDE)
    vmem = pl.BlockSpec(memory_space=pltpu.VMEM)
    hbm = pl.BlockSpec(memory_space=pl.ANY)
    f32, bf16 = jnp.float32, jnp.bfloat16
    waves = pltpu.VMEM((chunks, 3 * part, width), f32)
    results = pltpu.VMEM((peers, 8, part), f32)
    slots = pltpu.SemaphoreType.DMA((peers,))
    each = pltpu.SemaphoreType.DMA((chunks,))
    return pl.pallas_call(
        functools.partial(kernel, peers),
        out_shape=jax.ShapeDtypeStruct((peers, part), f32),
        in_specs=[hbm] * 8,
        out_specs=vmem,
        scratch_shapes=[
            pltpu.VMEM((beams, width), bf16),
            pltpu.VMEM((2 * beams, width), bf16),
            pltpu.VMEM(overlap.shape, f32),
            pltpu.VMEM((2, beams), f32),
            pltpu.VMEM((2, 4 * part, LANES), f32),
            pltpu.VMEM((peers, 2, here), jnp.int32),
            pltpu.VMEM((peers, 2 * per, pix), bf16),
            pltpu.VMEM((pix, width), bf16),
            waves, waves, waves, results, results,
            pltpu.VMEM((beams // LANES, LANES), f32),
            pltpu.VMEM((beams // LANES, LANES), f32),
            pltpu.VMEM(beam_k.shape, jnp.int32),
            pltpu.VMEM((1, patch_col.shape[0]), jnp.int32),
            pltpu.VMEM(patches.shape, bf16),
            pltpu.SemaphoreType.DMA((6,)),
            pltpu.SemaphoreType.DMA((4,)), pltpu.SemaphoreType.DMA((1,)),
            slots, slots, slots, slots, each, each, slots, slots,
        ],
        compiler_params=pltpu.CompilerParams(
            collective_id=0, has_side_effects=True, vmem_limit_bytes=56 << 20
        ),
    )(
        smatrix.reshape(beams, width),
        aperture.reshape(beams // LANES, LANES),
        aberration.reshape(beams // LANES, LANES),
        beam_k,
        probe_pos,
        patches,
        patch_col.reshape(1, patch_col.shape[0]),
        jnp.asarray(overlap),
    )


def solution(mesh):
    placed = (
        P(("grp", "beam"), "probe", None),
        P("beam"),
        P("beam"),
        P(None, "beam"),
        P(None, "probe"),
        P(("grp", "probe"), None),
        P("grp"),
    )
    whole = jax.shard_map(
        shards, mesh=mesh, in_specs=placed, out_specs=P("grp", ("probe", "beam")), check_vma=False
    )

    def run(*args):
        with jax.sharding.use_abstract_mesh(mesh.abstract_mesh):
            return whole(*args)

    return run
```

```python
import functools
import math

import jax
import jax.numpy as jnp
import numpy as np
from jax import lax
from jax.experimental import pallas as pl
from jax.experimental.pallas import tpu as pltpu
from jax.sharding import PartitionSpec as P

PSIDE = 16
GRID = 1024
LANES = 128
MESH = pl.DeviceIdType.MESH


def overlap_table(edge_count):
    half_side = edge_count // 2
    pixel = np.arange(edge_count * edge_count)
    mode = np.arange(edge_count * half_side)
    first = mode // half_side - half_side
    second = mode % half_side - edge_count // 4
    turns = np.mod(
        (pixel // edge_count)[:, None] * first[None, :]
        + (pixel % edge_count)[:, None] * second[None, :],
        edge_count,
    )
    angle = np.float32(2.0 * math.pi / edge_count) * turns.astype(np.float32)
    e_re = np.cos(angle).astype(jnp.bfloat16).astype(np.float64)
    e_im = (-np.sin(angle)).astype(jnp.bfloat16).astype(np.float64)
    g_re = e_re @ e_re.T + e_im @ e_im.T
    g_im = e_im @ e_re.T - e_re @ e_im.T
    return np.stack([g_re, g_im]).astype(np.float32)


def fraction(u):
    return u - jnp.round(u)


def cos_sin_turns(u):
    r = fraction(u)
    x = r * r
    s = r * (4.4428679 + x * (-7.3074434 + x * (3.5947879 + x * -0.7843736)))
    c = 1.4142041 + x * (-6.9776420 + x * (5.7152380 + x * -1.7283475))
    return 1.0 - s * s, s * c


COS_UNIT = 10.575109
SIN_UNIT = 16.216523


def scaled_cos_sin_turns(u):
    r = fraction(u)
    x = r * r
    s = r * ((x - 2.2338787) * x + 1.3657659)
    c = (x - 1.3820002) * x + 0.28310711
    return 0.094555356 - s * s, s * c


def ring_spot(index, peers):
    if peers != 8:
        return index
    line, along = lax.rem(index, 2), index // 2
    return along * (1 - line) + (peers - 1 - along) * line


def ring_index(spot, peers):
    if peers != 8:
        return spot
    line = spot // (peers // 2)
    return 2 * spot * (1 - line) + (2 * (peers - 1 - spot) + 1) * line


def chunk_order(peers):
    far = [d for d in range(3, peers - 2) if d != peers // 2] + [peers // 2, 2]
    pairs = [tuple(far[i : i + 2]) for i in range(0, len(far), 2)]
    return [(0,)] + pairs + [(peers - 2, 1, peers - 1)]


def kernel(
    peers, s_hbm, amp_hbm, aber_hbm, k_hbm, pos_hbm, pat_hbm, col_hbm, g_hbm, out_ref,
    s_v, w_v, g_v, kf, pb, posbuf, patbuf, nmat, psend, pown, precv, osend, orecv,
    amp_ref, aber_ref, k_ref, col_ref, pat_ref, m_sem, s_sem, g_sem, pos_ss, pos_rs, pat_ss, pat_rs, psi_ss, psi_rs, out_ss, out_rs,
):
    me = lax.axis_index("probe")
    core = lax.axis_index("beam")
    beams, width = s_v.shape
    pix = width // 2
    groups = beams // LANES
    part = posbuf.shape[2] // 2
    todo = chunk_order(peers)

    spot = ring_spot(me, peers)

    def at_offset(offset):
        return ring_index(lax.rem(spot + offset + peers, peers), peers)

    small = (
        (pos_hbm, posbuf.at[0]),
        (pat_hbm, pat_ref),
        (k_hbm, k_ref),
        (amp_hbm, amp_ref),
        (aber_hbm, aber_ref),
        (col_hbm, col_ref),
    )
    small = [pltpu.make_async_copy(x, y, m_sem.at[i]) for i, (x, y) in enumerate(small)]
    for copy in small:
        copy.start()
    pieces = s_sem.shape[0]
    piece = beams // pieces
    s_copies = [
        pltpu.make_async_copy(
            s_hbm.at[pl.ds(i * piece, piece)], s_v.at[pl.ds(i * piece, piece)], s_sem.at[i]
        )
        for i in range(pieces)
    ]
    for copy in s_copies:
        copy.start()
    g_copy = pltpu.make_async_copy(g_hbm, g_v, g_sem.at[0])
    g_copy.start()

    barrier = pltpu.get_barrier_semaphore()
    for offset in range(1, peers):
        pl.semaphore_signal(
            barrier, inc=1, device_id={"probe": at_offset(offset)}, device_id_type=MESH
        )
    pl.semaphore_signal(barrier, inc=1, device_id={"beam": 1 - core}, device_id_type=MESH)

    for copy in small:
        copy.wait()
    pat = pat_ref[...].astype(jnp.float32)
    patbuf[me] = jnp.concatenate([pat[:, :pix], pat[:, pix:]], axis=0).astype(jnp.bfloat16)
    kf[...] = k_ref[...].astype(jnp.float32) * (1.0 / GRID)
    amp = amp_ref[...] * COS_UNIT
    aber = aber_ref[...]
    aber_cos, aber_sin = cos_sin_turns(aber * (0.5 / math.pi))
    amp_cos = jnp.transpose(amp * aber_cos)
    amp_sin = jnp.transpose(amp * aber_sin)

    def position(offset, send):
        slot = peers - offset if send else offset
        return pltpu.make_async_remote_copy(
            src_ref=posbuf.at[0], dst_ref=posbuf.at[slot], send_sem=pos_ss.at[offset],
            recv_sem=pos_rs.at[slot], device_id={"probe": at_offset(offset)}, device_id_type=MESH,
        )

    def patch(offset, send):
        idx = me if send else at_offset(offset)
        return pltpu.make_async_remote_copy(
            src_ref=patbuf.at[idx], dst_ref=patbuf.at[idx], send_sem=pat_ss.at[offset],
            recv_sem=pat_rs.at[idx], device_id={"probe": at_offset(offset)}, device_id_type=MESH,
        )

    started = []

    def hand_out():
        pl.semaphore_wait(barrier, peers)
        receivers = [peers - o for offsets in todo for o in offsets if o]
        for move in (position, patch):
            for offset in receivers:
                copy = move(offset, True)
                copy.start()
                started.append(copy)

    ratio = SIN_UNIT / COS_UNIT
    for g in range(groups):
        if g * LANES % piece == 0:
            s_copies[g * LANES // piece].wait()
        s_blk = s_v[g * LANES : (g + 1) * LANES, :].astype(jnp.float32)
        s_re, s_im = s_blk[:, :pix], s_blk[:, pix:]
        fc, fs = amp_cos[:, g : g + 1], amp_sin[:, g : g + 1]
        c_re = fc * s_re + fs * s_im
        c_im = fc * s_im - fs * s_re
        base = 2 * g * LANES
        w_v[base : base + LANES, :pix] = c_re.astype(jnp.bfloat16)
        w_v[base : base + LANES, pix:] = c_im.astype(jnp.bfloat16)
        w_v[base + LANES : base + 2 * LANES, :pix] = (ratio * c_im).astype(jnp.bfloat16)
        w_v[base + LANES : base + 2 * LANES, pix:] = (-ratio * c_re).astype(jnp.bfloat16)
        if g == groups // pieces - 1:
            hand_out()

    def with_accumulators(body, rows, count):
        shapes = [pltpu.ACC(mxu)((rows, pix), jnp.float32) for mxu in (0, 1) for _ in range(count)]
        pl.run_scoped(lambda *accs: body(accs[:count], accs[count:]), *shapes)

    def columns(left, right, height):
        def group(g, carry):
            cols = pl.ds(pl.multiple_of(g * LANES, LANES), LANES)
            k1, k2 = kf[0:1, cols], kf[1:2, cols]
            wrows = pl.ds(pl.multiple_of(g * 2 * LANES, 2 * LANES), 2 * LANES)
            pltpu.matmul_push_rhs(w_v[wrows, :pix], 0, 0)
            pltpu.matmul_push_rhs(w_v[wrows, pix:], 0, 1)
            for n in range(len(left)):
                prow = pl.ds(n * height, height)
                cos_t, sin_t = scaled_cos_sin_turns(pb[0, prow, :] * k1 + pb[1, prow, :] * k2)
                lhs = jnp.concatenate(
                    [cos_t.astype(jnp.bfloat16), sin_t.astype(jnp.bfloat16)], axis=1
                )
                staged = 0 if n == 0 else None
                pltpu.matmul_acc_lhs(left[n], lhs, load_staged_rhs=staged)
                pltpu.matmul_acc_lhs(right[n], lhs, load_staged_rhs=staged)
            return carry

        lax.fori_loop(0, groups, group, 0, unroll=8)

    def psi_copy(i):
        span = pl.ds(0, len(todo[i]) * part)
        return pltpu.make_async_remote_copy(
            src_ref=psend.at[i, span], dst_ref=precv.at[i, span], send_sem=psi_ss.at[i],
            recv_sem=psi_rs.at[i], device_id={"beam": 1 - core}, device_id_type=MESH,
        )

    def waves(i, sides):
        offsets = todo[i]
        height = len(offsets) * part
        for j, offset in enumerate(offsets):
            if offset and 0 in sides:
                position(offset, False).wait_recv()
            for n, side in enumerate(sides):
                owner = core if side else 1 - core
                for t in range(part // LANES):
                    for axis in range(2):
                        lo = pl.multiple_of(owner * part + t * LANES, LANES)
                        line = posbuf[offset, axis : axis + 1, pl.ds(lo, LANES)]
                        row = n * height + j * part + t * LANES
                        pb[axis, row : row + LANES, :] = jnp.transpose(
                            jnp.broadcast_to(line.astype(jnp.float32), (LANES, LANES))
                        )

        def body(left, right):
            columns(left, right, height)
            for n, side in enumerate(sides):
                dst = pown if side else psend
                dst[i, :height, :pix] = pltpu.matmul_pop(left[n])
                dst[i, :height, pix:] = pltpu.matmul_pop(right[n])
                if not side:
                    copy.start()

        copy = psi_copy(i) if 0 in sides else None
        if copy:
            started.append(copy)
        with_accumulators(body, height, len(sides))

    def quadratic():
        for offset in range(1, peers):
            patch(offset, False).wait_recv()
        g_copy.wait()
        per = patbuf.shape[1] // 2
        p_all = patbuf[...].astype(jnp.float32)
        p_re = jnp.concatenate([p_all[d, :per] for d in range(peers)], axis=0)
        p_im = jnp.concatenate([p_all[d, per:] for d in range(peers)], axis=0)
        mine = jnp.where(col_ref[...] == me, 1.0, 0.0)
        lhs = jnp.concatenate([jnp.transpose(p_re) * mine, jnp.transpose(p_im) * mine], axis=1)
        rhs = jnp.concatenate(
            [jnp.concatenate([p_re, -p_im], axis=1), jnp.concatenate([p_im, p_re], axis=1)], axis=0
        )
        spare = -lhs.shape[1] % pix
        if spare:
            lhs = jnp.concatenate([lhs, jnp.zeros((pix, spare), jnp.float32)], axis=1)
            rhs = jnp.concatenate([rhs, jnp.zeros((spare, width), jnp.float32)], axis=0)
        lhs, rhs = lhs.astype(jnp.bfloat16), rhs.astype(jnp.bfloat16)
        def gram(left, right):
            for lo in range(0, lhs.shape[1], pix):
                pltpu.matmul_push_rhs(rhs[lo : lo + pix, :pix], 0, 0)
                pltpu.matmul_push_rhs(rhs[lo : lo + pix, pix:], 0, 1)
                pltpu.matmul_acc_lhs(left[0], lhs[:, lo : lo + pix], load_staged_rhs=0)
                pltpu.matmul_acc_lhs(right[0], lhs[:, lo : lo + pix], load_staged_rhs=0)
            store_form(pltpu.matmul_pop(left[0]), pltpu.matmul_pop(right[0]))

        with_accumulators(gram, pix, 1)

    def store_form(q_re, q_im):
        g_re, g_im = g_v[0], g_v[1]
        scale = 1.0 / float(pix * (pix // 2))
        m_re = (q_re * g_re - q_im * g_im) * scale
        m_im = (q_re * g_im + q_im * g_re) * (2.0 * scale)
        nmat[:, :pix] = m_re.astype(jnp.bfloat16)
        nmat[:, pix:] = m_im.astype(jnp.bfloat16)

    def result(offset, send):
        idx = at_offset(offset if send else -offset)
        return pltpu.make_async_remote_copy(
            src_ref=osend.at[offset], dst_ref=orecv.at[me if send else idx],
            send_sem=out_ss.at[offset], recv_sem=out_rs.at[me if send else idx],
            device_id={"probe": at_offset(offset)}, device_id_type=MESH,
        )

    def finish(i):
        offsets = todo[i]
        height = len(offsets) * part
        psi_copy(i).wait_recv()
        psi = (pown[i, :height] + precv[i, :height]).astype(jnp.bfloat16)
        a, b = psi[:, :pix], psi[:, pix:]

        def body(left, right):
            pltpu.matmul_push_rhs(nmat[:, :pix], 0, 0)
            pltpu.matmul_push_rhs(nmat[:, pix:], 0, 1)
            pltpu.matmul_acc_lhs(left[0], a, load_staged_rhs=0)
            pltpu.matmul_acc_lhs(right[0], a, load_staged_rhs=0)
            pltpu.matmul_push_rhs(nmat[:, :pix], 0, 1)
            pltpu.matmul_acc_lhs(right[0], b, load_staged_rhs=0)
            z = pltpu.matmul_pop(left[0]) * a.astype(jnp.float32)
            z += pltpu.matmul_pop(right[0]) * b.astype(jnp.float32)
            z = z[:, :LANES] + z[:, LANES:]
            for j, offset in enumerate(offsets):
                for t in range(0, part, LANES):
                    row = j * part + t
                    turned = jnp.transpose(z[row : row + LANES, :])
                    total = turned[0:8]
                    for lo in range(8, LANES, 8):
                        total += turned[lo : lo + 8]
                    osend[offset, :, t : t + LANES] = total
                if offset:
                    copies[j].start()

        copies = [result(offset, True) if offset else None for offset in offsets]
        started.extend(copy for copy in copies if copy)
        with_accumulators(body, height, 1)

    last = len(todo) - 1
    for i in range(last):
        waves(i, (0, 1))
        if i == 1:
            quadratic()
        if i >= 1:
            finish(i - 1)
    waves(last, (0,))
    finish(last - 1)
    waves(last, (1,))
    finish(last)
    orecv[me] = osend[0]
    for offset in range(1, peers):
        result(offset, False).wait_recv()
    out_ref[...] = jnp.sum(orecv[...], axis=1)
    for copy in started:
        copy.wait_send()


def shards(smatrix, aperture, aberration, beam_k, probe_pos, patches, patch_col):
    peers = lax.axis_size("probe")
    beams, _, width = smatrix.shape
    here = probe_pos.shape[1]
    part = here // lax.axis_size("beam")
    per = patches.shape[0]
    pix = width // 2
    chunks = len(chunk_order(peers))
    overlap = overlap_table(PSIDE)
    vmem = pl.BlockSpec(memory_space=pltpu.VMEM)
    hbm = pl.BlockSpec(memory_space=pl.ANY)
    f32, bf16 = jnp.float32, jnp.bfloat16
    waves = pltpu.VMEM((chunks, 3 * part, width), f32)
    results = pltpu.VMEM((peers, 8, part), f32)
    slots = pltpu.SemaphoreType.DMA((peers,))
    each = pltpu.SemaphoreType.DMA((chunks,))
    return pl.pallas_call(
        functools.partial(kernel, peers),
        out_shape=jax.ShapeDtypeStruct((peers, part), f32),
        in_specs=[hbm] * 8,
        out_specs=vmem,
        scratch_shapes=[
            pltpu.VMEM((beams, width), bf16),
            pltpu.VMEM((2 * beams, width), bf16),
            pltpu.VMEM(overlap.shape, f32),
            pltpu.VMEM((2, beams), f32),
            pltpu.VMEM((2, 4 * part, LANES), f32),
            pltpu.VMEM((peers, 2, here), jnp.int32),
            pltpu.VMEM((peers, 2 * per, pix), bf16),
            pltpu.VMEM((pix, width), bf16),
            waves, waves, waves, results, results,
            pltpu.VMEM((beams // LANES, LANES), f32),
            pltpu.VMEM((beams // LANES, LANES), f32),
            pltpu.VMEM(beam_k.shape, jnp.int32),
            pltpu.VMEM((1, patch_col.shape[0]), jnp.int32),
            pltpu.VMEM(patches.shape, bf16),
            pltpu.SemaphoreType.DMA((6,)),
            pltpu.SemaphoreType.DMA((4,)), pltpu.SemaphoreType.DMA((1,)),
            slots, slots, slots, slots, each, each, slots, slots,
        ],
        compiler_params=pltpu.CompilerParams(
            collective_id=0, has_side_effects=True, vmem_limit_bytes=56 << 20
        ),
    )(
        smatrix.reshape(beams, width),
        aperture.reshape(beams // LANES, LANES),
        aberration.reshape(beams // LANES, LANES),
        beam_k,
        probe_pos,
        patches,
        patch_col.reshape(1, patch_col.shape[0]),
        jnp.asarray(overlap),
    )


def solution(mesh):
    placed = (
        P(("grp", "beam"), "probe", None),
        P("beam"),
        P("beam"),
        P(None, "beam"),
        P(None, "probe"),
        P(("grp", "probe"), None),
        P("grp"),
    )
    whole = jax.shard_map(
        shards, mesh=mesh, in_specs=placed, out_specs=P("grp", ("probe", "beam")), check_vma=False
    )

    def run(*args):
        with jax.sharding.use_abstract_mesh(mesh.abstract_mesh):
            return whole(*args)

    return run
```

```python
import functools
import math

import jax
import jax.numpy as jnp
import numpy as np
from jax import lax
from jax.experimental import pallas as pl
from jax.experimental.pallas import tpu as pltpu
from jax.sharding import PartitionSpec as P

PSIDE = 16
GRID = 1024
LANES = 128
MESH = pl.DeviceIdType.MESH


def overlap_table(edge_count):
    half_side = edge_count // 2
    pixel = np.arange(edge_count * edge_count)
    mode = np.arange(edge_count * half_side)
    first = mode // half_side - half_side
    second = mode % half_side - edge_count // 4
    turns = np.mod(
        (pixel // edge_count)[:, None] * first[None, :]
        + (pixel % edge_count)[:, None] * second[None, :],
        edge_count,
    )
    angle = np.float32(2.0 * math.pi / edge_count) * turns.astype(np.float32)
    e_re = np.cos(angle).astype(jnp.bfloat16).astype(np.float64)
    e_im = (-np.sin(angle)).astype(jnp.bfloat16).astype(np.float64)
    g_re = e_re @ e_re.T + e_im @ e_im.T
    g_im = e_im @ e_re.T - e_re @ e_im.T
    return np.stack([g_re, g_im]).astype(np.float32)


def fraction(u):
    return u - jnp.round(u)


def cos_sin_turns(u):
    r = fraction(u)
    x = r * r
    s = r * (4.4428679 + x * (-7.3074434 + x * (3.5947879 + x * -0.7843736)))
    c = 1.4142041 + x * (-6.9776420 + x * (5.7152380 + x * -1.7283475))
    return 1.0 - s * s, s * c


COS_UNIT = 10.575109
SIN_UNIT = 16.216523


def scaled_cos_sin_turns(u):
    r = fraction(u)
    x = r * r
    s = r * ((x - 2.2338787) * x + 1.3657659)
    c = (x - 1.3820002) * x + 0.28310711
    return 0.094555356 - s * s, s * c


def ring_spot(index, peers):
    if peers != 8:
        return index
    line, along = lax.rem(index, 2), index // 2
    return along * (1 - line) + (peers - 1 - along) * line


def ring_index(spot, peers):
    if peers != 8:
        return spot
    line = spot // (peers // 2)
    return 2 * spot * (1 - line) + (2 * (peers - 1 - spot) + 1) * line


def chunk_order(peers):
    far = [d for d in range(3, peers - 2) if d != peers // 2] + [peers // 2, 2]
    pairs = [tuple(far[i : i + 2]) for i in range(0, len(far), 2)]
    return [(0,)] + pairs + [(peers - 2, 1, peers - 1)]


def kernel(
    peers, s_hbm, amp_hbm, aber_hbm, k_hbm, pos_hbm, pat_hbm, col_hbm, g_hbm, out_ref,
    s_v, w_v, g_v, kf, pb, posbuf, patbuf, nmat, psend, pown, precv, osend, orecv,
    amp_ref, aber_ref, k_ref, col_ref, pat_ref, m_sem, s_sem, g_sem, pos_ss, pos_rs, pat_ss, pat_rs, psi_ss, psi_rs, out_ss, out_rs,
):
    me = lax.axis_index("probe")
    core = lax.axis_index("beam")
    beams, width = s_v.shape
    pix = width // 2
    groups = beams // LANES
    part = posbuf.shape[2] // 2
    todo = chunk_order(peers)

    spot = ring_spot(me, peers)

    def at_offset(offset):
        return ring_index(lax.rem(spot + offset + peers, peers), peers)

    small = (
        (pos_hbm, posbuf.at[0]),
        (pat_hbm, pat_ref),
        (k_hbm, k_ref),
        (amp_hbm, amp_ref),
        (aber_hbm, aber_ref),
        (col_hbm, col_ref),
    )
    small = [pltpu.make_async_copy(x, y, m_sem.at[i]) for i, (x, y) in enumerate(small)]
    for copy in small:
        copy.start()
    pieces = s_sem.shape[0]
    piece = beams // pieces
    s_copies = [
        pltpu.make_async_copy(
            s_hbm.at[pl.ds(i * piece, piece)], s_v.at[pl.ds(i * piece, piece)], s_sem.at[i]
        )
        for i in range(pieces)
    ]
    for copy in s_copies:
        copy.start()
    g_copy = pltpu.make_async_copy(g_hbm, g_v, g_sem.at[0])
    g_copy.start()

    barrier = pltpu.get_barrier_semaphore()
    for offset in range(1, peers):
        pl.semaphore_signal(
            barrier, inc=1, device_id={"probe": at_offset(offset)}, device_id_type=MESH
        )
    pl.semaphore_signal(barrier, inc=1, device_id={"beam": 1 - core}, device_id_type=MESH)

    for copy in small:
        copy.wait()
    pat = pat_ref[...].astype(jnp.float32)
    patbuf[me] = jnp.concatenate([pat[:, :pix], pat[:, pix:]], axis=0).astype(jnp.bfloat16)
    kf[...] = k_ref[...].astype(jnp.float32) * (1.0 / GRID)
    amp = amp_ref[...] * COS_UNIT
    aber = aber_ref[...]
    aber_cos, aber_sin = cos_sin_turns(aber * (0.5 / math.pi))
    amp_cos = jnp.transpose(amp * aber_cos)
    amp_sin = jnp.transpose(amp * aber_sin)

    def position(offset, send):
        slot = peers - offset if send else offset
        return pltpu.make_async_remote_copy(
            src_ref=posbuf.at[0], dst_ref=posbuf.at[slot], send_sem=pos_ss.at[offset],
            recv_sem=pos_rs.at[slot], device_id={"probe": at_offset(offset)}, device_id_type=MESH,
        )

    def patch(offset, send):
        idx = me if send else at_offset(offset)
        return pltpu.make_async_remote_copy(
            src_ref=patbuf.at[idx], dst_ref=patbuf.at[idx], send_sem=pat_ss.at[offset],
            recv_sem=pat_rs.at[idx], device_id={"probe": at_offset(offset)}, device_id_type=MESH,
        )

    started = []

    def hand_out():
        pl.semaphore_wait(barrier, peers)
        receivers = [peers - o for offsets in todo for o in offsets if o]
        for move in (position, patch):
            for offset in receivers:
                copy = move(offset, True)
                copy.start()
                started.append(copy)

    ratio = SIN_UNIT / COS_UNIT
    for g in range(groups):
        if g * LANES % piece == 0:
            s_copies[g * LANES // piece].wait()
        s_blk = s_v[g * LANES : (g + 1) * LANES, :].astype(jnp.float32)
        s_re, s_im = s_blk[:, :pix], s_blk[:, pix:]
        fc, fs = amp_cos[:, g : g + 1], amp_sin[:, g : g + 1]
        c_re = fc * s_re + fs * s_im
        c_im = fc * s_im - fs * s_re
        base = 2 * g * LANES
        w_v[base : base + LANES, :pix] = c_re.astype(jnp.bfloat16)
        w_v[base : base + LANES, pix:] = c_im.astype(jnp.bfloat16)
        w_v[base + LANES : base + 2 * LANES, :pix] = (ratio * c_im).astype(jnp.bfloat16)
        w_v[base + LANES : base + 2 * LANES, pix:] = (-ratio * c_re).astype(jnp.bfloat16)
        if g == groups // pieces - 1:
            hand_out()

    def with_accumulators(body, rows, count):
        shapes = [pltpu.ACC(mxu)((rows, pix), jnp.float32) for mxu in (0, 1) for _ in range(count)]
        pl.run_scoped(lambda *accs: body(accs[:count], accs[count:]), *shapes)

    def columns(left, right, height):
        def group(g, carry):
            cols = pl.ds(pl.multiple_of(g * LANES, LANES), LANES)
            k1, k2 = kf[0:1, cols], kf[1:2, cols]
            wrows = pl.ds(pl.multiple_of(g * 2 * LANES, 2 * LANES), 2 * LANES)
            pltpu.matmul_push_rhs(w_v[wrows, :pix], 0, 0)
            pltpu.matmul_push_rhs(w_v[wrows, pix:], 0, 1)
            for n in range(len(left)):
                prow = pl.ds(n * height, height)
                cos_t, sin_t = scaled_cos_sin_turns(pb[0, prow, :] * k1 + pb[1, prow, :] * k2)
                lhs = jnp.concatenate(
                    [cos_t.astype(jnp.bfloat16), sin_t.astype(jnp.bfloat16)], axis=1
                )
                staged = 0 if n == 0 else None
                pltpu.matmul_acc_lhs(left[n], lhs, load_staged_rhs=staged)
                pltpu.matmul_acc_lhs(right[n], lhs, load_staged_rhs=staged)
            return carry

        lax.fori_loop(0, groups, group, 0, unroll=8)

    def psi_copy(i):
        span = pl.ds(0, len(todo[i]) * part)
        return pltpu.make_async_remote_copy(
            src_ref=psend.at[i, span], dst_ref=precv.at[i, span], send_sem=psi_ss.at[i],
            recv_sem=psi_rs.at[i], device_id={"beam": 1 - core}, device_id_type=MESH,
        )

    def waves(i, sides):
        offsets = todo[i]
        height = len(offsets) * part
        for j, offset in enumerate(offsets):
            if offset and 0 in sides:
                position(offset, False).wait_recv()
            for n, side in enumerate(sides):
                owner = core if side else 1 - core
                for t in range(part // LANES):
                    for axis in range(2):
                        lo = pl.multiple_of(owner * part + t * LANES, LANES)
                        line = posbuf[offset, axis : axis + 1, pl.ds(lo, LANES)]
                        row = n * height + j * part + t * LANES
                        pb[axis, row : row + LANES, :] = jnp.transpose(
                            jnp.broadcast_to(line.astype(jnp.float32), (LANES, LANES))
                        )

        def body(left, right):
            columns(left, right, height)
            for n, side in enumerate(sides):
                dst = pown if side else psend
                dst[i, :height, :pix] = pltpu.matmul_pop(left[n]).astype(dst.dtype)
                dst[i, :height, pix:] = pltpu.matmul_pop(right[n]).astype(dst.dtype)
                if not side:
                    copy.start()

        copy = psi_copy(i) if 0 in sides else None
        if copy:
            started.append(copy)
        with_accumulators(body, height, len(sides))

    def quadratic():
        for offset in range(1, peers):
            patch(offset, False).wait_recv()
        g_copy.wait()
        per = patbuf.shape[1] // 2
        p_all = patbuf[...].astype(jnp.float32)
        p_re = jnp.concatenate([p_all[d, :per] for d in range(peers)], axis=0)
        p_im = jnp.concatenate([p_all[d, per:] for d in range(peers)], axis=0)
        mine = jnp.where(col_ref[...] == me, 1.0, 0.0)
        lhs = jnp.concatenate([jnp.transpose(p_re) * mine, jnp.transpose(p_im) * mine], axis=1)
        rhs = jnp.concatenate(
            [jnp.concatenate([p_re, -p_im], axis=1), jnp.concatenate([p_im, p_re], axis=1)], axis=0
        )
        spare = -lhs.shape[1] % pix
        if spare:
            lhs = jnp.concatenate([lhs, jnp.zeros((pix, spare), jnp.float32)], axis=1)
            rhs = jnp.concatenate([rhs, jnp.zeros((spare, width), jnp.float32)], axis=0)
        lhs, rhs = lhs.astype(jnp.bfloat16), rhs.astype(jnp.bfloat16)
        def gram(left, right):
            for lo in range(0, lhs.shape[1], pix):
                pltpu.matmul_push_rhs(rhs[lo : lo + pix, :pix], 0, 0)
                pltpu.matmul_push_rhs(rhs[lo : lo + pix, pix:], 0, 1)
                pltpu.matmul_acc_lhs(left[0], lhs[:, lo : lo + pix], load_staged_rhs=0)
                pltpu.matmul_acc_lhs(right[0], lhs[:, lo : lo + pix], load_staged_rhs=0)
            store_form(pltpu.matmul_pop(left[0]), pltpu.matmul_pop(right[0]))

        with_accumulators(gram, pix, 1)

    def store_form(q_re, q_im):
        g_re, g_im = g_v[0], g_v[1]
        scale = 1.0 / float(pix * (pix // 2))
        m_re = (q_re * g_re - q_im * g_im) * scale
        m_im = (q_re * g_im + q_im * g_re) * (2.0 * scale)
        nmat[:, :pix] = m_re.astype(jnp.bfloat16)
        nmat[:, pix:] = m_im.astype(jnp.bfloat16)

    def result(offset, send):
        idx = at_offset(offset if send else -offset)
        return pltpu.make_async_remote_copy(
            src_ref=osend.at[offset], dst_ref=orecv.at[me if send else idx],
            send_sem=out_ss.at[offset], recv_sem=out_rs.at[me if send else idx],
            device_id={"probe": at_offset(offset)}, device_id_type=MESH,
        )

    def finish(i):
        offsets = todo[i]
        height = len(offsets) * part
        psi_copy(i).wait_recv()
        psi = (pown[i, :height] + precv[i, :height].astype(jnp.float32)).astype(jnp.bfloat16)
        a, b = psi[:, :pix], psi[:, pix:]

        def body(left, right):
            pltpu.matmul_push_rhs(nmat[:, :pix], 0, 0)
            pltpu.matmul_push_rhs(nmat[:, pix:], 0, 1)
            pltpu.matmul_acc_lhs(left[0], a, load_staged_rhs=0)
            pltpu.matmul_acc_lhs(right[0], a, load_staged_rhs=0)
            pltpu.matmul_push_rhs(nmat[:, :pix], 0, 1)
            pltpu.matmul_acc_lhs(right[0], b, load_staged_rhs=0)
            z = pltpu.matmul_pop(left[0]) * a.astype(jnp.float32)
            z += pltpu.matmul_pop(right[0]) * b.astype(jnp.float32)
            z = z[:, :LANES] + z[:, LANES:]
            for j, offset in enumerate(offsets):
                for t in range(0, part, LANES):
                    row = j * part + t
                    turned = jnp.transpose(z[row : row + LANES, :])
                    total = turned[0:8]
                    for lo in range(8, LANES, 8):
                        total += turned[lo : lo + 8]
                    osend[offset, :, t : t + LANES] = total
                if offset:
                    copies[j].start()

        copies = [result(offset, True) if offset else None for offset in offsets]
        started.extend(copy for copy in copies if copy)
        with_accumulators(body, height, 1)

    last = len(todo) - 1
    for i in range(last):
        waves(i, (0, 1))
        if i == 1:
            quadratic()
        if i >= 1:
            finish(i - 1)
    waves(last, (0,))
    finish(last - 1)
    waves(last, (1,))
    finish(last)
    orecv[me] = osend[0]
    for offset in range(1, peers):
        result(offset, False).wait_recv()
    out_ref[...] = jnp.sum(orecv[...], axis=1)
    for copy in started:
        copy.wait_send()


def shards(smatrix, aperture, aberration, beam_k, probe_pos, patches, patch_col):
    peers = lax.axis_size("probe")
    beams, _, width = smatrix.shape
    here = probe_pos.shape[1]
    part = here // lax.axis_size("beam")
    per = patches.shape[0]
    pix = width // 2
    chunks = len(chunk_order(peers))
    overlap = overlap_table(PSIDE)
    vmem = pl.BlockSpec(memory_space=pltpu.VMEM)
    hbm = pl.BlockSpec(memory_space=pl.ANY)
    f32, bf16 = jnp.float32, jnp.bfloat16
    waves = pltpu.VMEM((chunks, 3 * part, width), f32)
    sent_waves = pltpu.VMEM((chunks, 3 * part, width), bf16)
    results = pltpu.VMEM((peers, 8, part), f32)
    slots = pltpu.SemaphoreType.DMA((peers,))
    each = pltpu.SemaphoreType.DMA((chunks,))
    return pl.pallas_call(
        functools.partial(kernel, peers),
        out_shape=jax.ShapeDtypeStruct((peers, part), f32),
        in_specs=[hbm] * 8,
        out_specs=vmem,
        scratch_shapes=[
            pltpu.VMEM((beams, width), bf16),
            pltpu.VMEM((2 * beams, width), bf16),
            pltpu.VMEM(overlap.shape, f32),
            pltpu.VMEM((2, beams), f32),
            pltpu.VMEM((2, 4 * part, LANES), f32),
            pltpu.VMEM((peers, 2, here), jnp.int32),
            pltpu.VMEM((peers, 2 * per, pix), bf16),
            pltpu.VMEM((pix, width), bf16),
            sent_waves, waves, sent_waves, results, results,
            pltpu.VMEM((beams // LANES, LANES), f32),
            pltpu.VMEM((beams // LANES, LANES), f32),
            pltpu.VMEM(beam_k.shape, jnp.int32),
            pltpu.VMEM((1, patch_col.shape[0]), jnp.int32),
            pltpu.VMEM(patches.shape, bf16),
            pltpu.SemaphoreType.DMA((6,)),
            pltpu.SemaphoreType.DMA((4,)), pltpu.SemaphoreType.DMA((1,)),
            slots, slots, slots, slots, each, each, slots, slots,
        ],
        compiler_params=pltpu.CompilerParams(
            collective_id=0, has_side_effects=True, vmem_limit_bytes=56 << 20
        ),
    )(
        smatrix.reshape(beams, width),
        aperture.reshape(beams // LANES, LANES),
        aberration.reshape(beams // LANES, LANES),
        beam_k,
        probe_pos,
        patches,
        patch_col.reshape(1, patch_col.shape[0]),
        jnp.asarray(overlap),
    )


def solution(mesh):
    placed = (
        P(("grp", "beam"), "probe", None),
        P("beam"),
        P("beam"),
        P(None, "beam"),
        P(None, "probe"),
        P(("grp", "probe"), None),
        P("grp"),
    )
    whole = jax.shard_map(
        shards, mesh=mesh, in_specs=placed, out_specs=P("grp", ("probe", "beam")), check_vma=False
    )

    def run(*args):
        with jax.sharding.use_abstract_mesh(mesh.abstract_mesh):
            return whole(*args)

    return run
```

```python
import functools
import math

import jax
import jax.numpy as jnp
import numpy as np
from jax import lax
from jax.experimental import pallas as pl
from jax.experimental.pallas import tpu as pltpu
from jax.sharding import PartitionSpec as P

PSIDE = 16
GRID = 1024
LANES = 128
MESH = pl.DeviceIdType.MESH


def overlap_table(edge_count):
    half_side = edge_count // 2
    pixel = np.arange(edge_count * edge_count)
    mode = np.arange(edge_count * half_side)
    first = mode // half_side - half_side
    second = mode % half_side - edge_count // 4
    turns = np.mod(
        (pixel // edge_count)[:, None] * first[None, :]
        + (pixel % edge_count)[:, None] * second[None, :],
        edge_count,
    )
    angle = np.float32(2.0 * math.pi / edge_count) * turns.astype(np.float32)
    e_re = np.cos(angle).astype(jnp.bfloat16).astype(np.float64)
    e_im = (-np.sin(angle)).astype(jnp.bfloat16).astype(np.float64)
    g_re = e_re @ e_re.T + e_im @ e_im.T
    g_im = e_im @ e_re.T - e_re @ e_im.T
    return np.stack([g_re, g_im]).astype(np.float32)


def fraction(u):
    return u - jnp.round(u)


def cos_sin_turns(u):
    r = fraction(u)
    x = r * r
    s = r * (4.4428679 + x * (-7.3074434 + x * (3.5947879 + x * -0.7843736)))
    c = 1.4142041 + x * (-6.9776420 + x * (5.7152380 + x * -1.7283475))
    return 1.0 - s * s, s * c


COS_UNIT = 10.575109
SIN_UNIT = 16.216523


def scaled_cos_sin_turns(u):
    r = fraction(u)
    x = r * r
    s = r * ((x - 2.2338787) * x + 1.3657659)
    c = (x - 1.3820002) * x + 0.28310711
    return 0.094555356 - s * s, s * c


def ring_spot(index, peers):
    if peers != 8:
        return index
    line, along = lax.rem(index, 2), index // 2
    return along * (1 - line) + (peers - 1 - along) * line


def ring_index(spot, peers):
    if peers != 8:
        return spot
    line = spot // (peers // 2)
    return 2 * spot * (1 - line) + (2 * (peers - 1 - spot) + 1) * line


def chunk_order(peers):
    far = [d for d in range(3, peers - 2) if d != peers // 2] + [peers // 2, 2]
    pairs = [tuple(far[i : i + 2]) for i in range(0, len(far), 2)]
    return [(0, 1)] + pairs + [(peers - 2, peers - 1)]


def kernel(
    peers, s_hbm, amp_hbm, aber_hbm, k_hbm, pos_hbm, pat_hbm, col_hbm, g_hbm, out_ref,
    s_v, w_v, g_v, kf, pb, posbuf, patbuf, nmat, psend, pown, precv, osend, orecv,
    amp_ref, aber_ref, k_ref, col_ref, pat_ref, m_sem, s_sem, g_sem, pos_ss, pos_rs, pat_ss, pat_rs, psi_ss, psi_rs, out_ss, out_rs,
):
    me = lax.axis_index("probe")
    core = lax.axis_index("beam")
    beams, width = s_v.shape
    pix = width // 2
    groups = beams // LANES
    part = posbuf.shape[2] // 2
    todo = chunk_order(peers)

    spot = ring_spot(me, peers)

    def at_offset(offset):
        return ring_index(lax.rem(spot + offset + peers, peers), peers)

    small = (
        (pos_hbm, posbuf.at[0]),
        (pat_hbm, pat_ref),
        (k_hbm, k_ref),
        (amp_hbm, amp_ref),
        (aber_hbm, aber_ref),
        (col_hbm, col_ref),
    )
    small = [pltpu.make_async_copy(x, y, m_sem.at[i]) for i, (x, y) in enumerate(small)]
    for copy in small:
        copy.start()
    pieces = s_sem.shape[0]
    piece = beams // pieces
    s_copies = [
        pltpu.make_async_copy(
            s_hbm.at[pl.ds(i * piece, piece)], s_v.at[pl.ds(i * piece, piece)], s_sem.at[i]
        )
        for i in range(pieces)
    ]
    for copy in s_copies:
        copy.start()
    g_copy = pltpu.make_async_copy(g_hbm, g_v, g_sem.at[0])
    g_copy.start()

    barrier = pltpu.get_barrier_semaphore()
    for offset in range(1, peers):
        pl.semaphore_signal(
            barrier, inc=1, device_id={"probe": at_offset(offset)}, device_id_type=MESH
        )
    pl.semaphore_signal(barrier, inc=1, device_id={"beam": 1 - core}, device_id_type=MESH)

    for copy in small:
        copy.wait()
    pat = pat_ref[...].astype(jnp.float32)
    patbuf[me] = jnp.concatenate([pat[:, :pix], pat[:, pix:]], axis=0).astype(jnp.bfloat16)
    kf[...] = k_ref[...].astype(jnp.float32) * (1.0 / GRID)
    amp = amp_ref[...] * COS_UNIT
    aber = aber_ref[...]
    aber_cos, aber_sin = cos_sin_turns(aber * (0.5 / math.pi))
    amp_cos = jnp.transpose(amp * aber_cos)
    amp_sin = jnp.transpose(amp * aber_sin)

    def position(offset, send):
        slot = peers - offset if send else offset
        return pltpu.make_async_remote_copy(
            src_ref=posbuf.at[0], dst_ref=posbuf.at[slot], send_sem=pos_ss.at[offset],
            recv_sem=pos_rs.at[slot], device_id={"probe": at_offset(offset)}, device_id_type=MESH,
        )

    def patch(offset, send):
        idx = me if send else at_offset(offset)
        return pltpu.make_async_remote_copy(
            src_ref=patbuf.at[idx], dst_ref=patbuf.at[idx], send_sem=pat_ss.at[offset],
            recv_sem=pat_rs.at[idx], device_id={"probe": at_offset(offset)}, device_id_type=MESH,
        )

    started = []

    def hand_out():
        pl.semaphore_wait(barrier, peers)
        receivers = [peers - o for offsets in todo for o in offsets if o]
        for move in (position, patch):
            for offset in receivers:
                copy = move(offset, True)
                copy.start()
                started.append(copy)

    hand_out()

    ratio = SIN_UNIT / COS_UNIT
    for g in range(groups):
        if g * LANES % piece == 0:
            s_copies[g * LANES // piece].wait()
        s_blk = s_v[g * LANES : (g + 1) * LANES, :].astype(jnp.float32)
        s_re, s_im = s_blk[:, :pix], s_blk[:, pix:]
        fc, fs = amp_cos[:, g : g + 1], amp_sin[:, g : g + 1]
        c_re = fc * s_re + fs * s_im
        c_im = fc * s_im - fs * s_re
        base = 2 * g * LANES
        w_v[base : base + LANES, :pix] = c_re.astype(jnp.bfloat16)
        w_v[base : base + LANES, pix:] = c_im.astype(jnp.bfloat16)
        w_v[base + LANES : base + 2 * LANES, :pix] = (ratio * c_im).astype(jnp.bfloat16)
        w_v[base + LANES : base + 2 * LANES, pix:] = (-ratio * c_re).astype(jnp.bfloat16)

    def with_accumulators(body, rows, count):
        shapes = [pltpu.ACC(mxu)((rows, pix), jnp.float32) for mxu in (0, 1) for _ in range(count)]
        pl.run_scoped(lambda *accs: body(accs[:count], accs[count:]), *shapes)

    def columns(left, right, height):
        def group(g, carry):
            cols = pl.ds(pl.multiple_of(g * LANES, LANES), LANES)
            k1, k2 = kf[0:1, cols], kf[1:2, cols]
            wrows = pl.ds(pl.multiple_of(g * 2 * LANES, 2 * LANES), 2 * LANES)
            pltpu.matmul_push_rhs(w_v[wrows, :pix], 0, 0)
            pltpu.matmul_push_rhs(w_v[wrows, pix:], 0, 1)
            for n in range(len(left)):
                prow = pl.ds(n * height, height)
                cos_t, sin_t = scaled_cos_sin_turns(pb[0, prow, :] * k1 + pb[1, prow, :] * k2)
                lhs = jnp.concatenate(
                    [cos_t.astype(jnp.bfloat16), sin_t.astype(jnp.bfloat16)], axis=1
                )
                staged = 0 if n == 0 else None
                pltpu.matmul_acc_lhs(left[n], lhs, load_staged_rhs=staged)
                pltpu.matmul_acc_lhs(right[n], lhs, load_staged_rhs=staged)
            return carry

        lax.fori_loop(0, groups, group, 0, unroll=8)

    def psi_copy(i):
        span = pl.ds(0, len(todo[i]) * part)
        return pltpu.make_async_remote_copy(
            src_ref=psend.at[i, span], dst_ref=precv.at[i, span], send_sem=psi_ss.at[i],
            recv_sem=psi_rs.at[i], device_id={"beam": 1 - core}, device_id_type=MESH,
        )

    def waves(i, sides):
        offsets = todo[i]
        height = len(offsets) * part
        for j, offset in enumerate(offsets):
            if offset and 0 in sides:
                position(offset, False).wait_recv()
            for n, side in enumerate(sides):
                owner = core if side else 1 - core
                for t in range(part // LANES):
                    for axis in range(2):
                        lo = pl.multiple_of(owner * part + t * LANES, LANES)
                        line = posbuf[offset, axis : axis + 1, pl.ds(lo, LANES)]
                        row = n * height + j * part + t * LANES
                        pb[axis, row : row + LANES, :] = jnp.transpose(
                            jnp.broadcast_to(line.astype(jnp.float32), (LANES, LANES))
                        )

        def body(left, right):
            columns(left, right, height)
            for n, side in enumerate(sides):
                dst = pown if side else psend
                dst[i, :height, :pix] = pltpu.matmul_pop(left[n])
                dst[i, :height, pix:] = pltpu.matmul_pop(right[n])
                if not side:
                    copy.start()

        copy = psi_copy(i) if 0 in sides else None
        if copy:
            started.append(copy)
        with_accumulators(body, height, len(sides))

    def quadratic():
        for offset in range(1, peers):
            patch(offset, False).wait_recv()
        g_copy.wait()
        per = patbuf.shape[1] // 2
        p_all = patbuf[...].astype(jnp.float32)
        p_re = jnp.concatenate([p_all[d, :per] for d in range(peers)], axis=0)
        p_im = jnp.concatenate([p_all[d, per:] for d in range(peers)], axis=0)
        mine = jnp.where(col_ref[...] == me, 1.0, 0.0)
        lhs = jnp.concatenate([jnp.transpose(p_re) * mine, jnp.transpose(p_im) * mine], axis=1)
        rhs = jnp.concatenate(
            [jnp.concatenate([p_re, -p_im], axis=1), jnp.concatenate([p_im, p_re], axis=1)], axis=0
        )
        spare = -lhs.shape[1] % pix
        if spare:
            lhs = jnp.concatenate([lhs, jnp.zeros((pix, spare), jnp.float32)], axis=1)
            rhs = jnp.concatenate([rhs, jnp.zeros((spare, width), jnp.float32)], axis=0)
        lhs, rhs = lhs.astype(jnp.bfloat16), rhs.astype(jnp.bfloat16)
        def gram(left, right):
            for lo in range(0, lhs.shape[1], pix):
                pltpu.matmul_push_rhs(rhs[lo : lo + pix, :pix], 0, 0)
                pltpu.matmul_push_rhs(rhs[lo : lo + pix, pix:], 0, 1)
                pltpu.matmul_acc_lhs(left[0], lhs[:, lo : lo + pix], load_staged_rhs=0)
                pltpu.matmul_acc_lhs(right[0], lhs[:, lo : lo + pix], load_staged_rhs=0)
            store_form(pltpu.matmul_pop(left[0]), pltpu.matmul_pop(right[0]))

        with_accumulators(gram, pix, 1)

    def store_form(q_re, q_im):
        g_re, g_im = g_v[0], g_v[1]
        scale = 1.0 / float(pix * (pix // 2))
        m_re = (q_re * g_re - q_im * g_im) * scale
        m_im = (q_re * g_im + q_im * g_re) * (2.0 * scale)
        nmat[:, :pix] = m_re.astype(jnp.bfloat16)
        nmat[:, pix:] = m_im.astype(jnp.bfloat16)

    def result(offset, send):
        idx = at_offset(offset if send else -offset)
        return pltpu.make_async_remote_copy(
            src_ref=osend.at[offset], dst_ref=orecv.at[me if send else idx],
            send_sem=out_ss.at[offset], recv_sem=out_rs.at[me if send else idx],
            device_id={"probe": at_offset(offset)}, device_id_type=MESH,
        )

    def finish(i):
        offsets = todo[i]
        height = len(offsets) * part
        psi_copy(i).wait_recv()
        psi = (pown[i, :height] + precv[i, :height]).astype(jnp.bfloat16)
        a, b = psi[:, :pix], psi[:, pix:]

        def body(left, right):
            pltpu.matmul_push_rhs(nmat[:, :pix], 0, 0)
            pltpu.matmul_push_rhs(nmat[:, pix:], 0, 1)
            pltpu.matmul_acc_lhs(left[0], a, load_staged_rhs=0)
            pltpu.matmul_acc_lhs(right[0], a, load_staged_rhs=0)
            pltpu.matmul_push_rhs(nmat[:, :pix], 0, 1)
            pltpu.matmul_acc_lhs(right[0], b, load_staged_rhs=0)
            z = pltpu.matmul_pop(left[0]) * a.astype(jnp.float32)
            z += pltpu.matmul_pop(right[0]) * b.astype(jnp.float32)
            z = z[:, :LANES] + z[:, LANES:]
            for j, offset in enumerate(offsets):
                for t in range(0, part, LANES):
                    row = j * part + t
                    turned = jnp.transpose(z[row : row + LANES, :])
                    total = turned[0:8]
                    for lo in range(8, LANES, 8):
                        total += turned[lo : lo + 8]
                    osend[offset, :, t : t + LANES] = total
                if offset:
                    copies[j].start()

        copies = [result(offset, True) if offset else None for offset in offsets]
        started.extend(copy for copy in copies if copy)
        with_accumulators(body, height, 1)

    last = len(todo) - 1
    for i in range(last):
        waves(i, (0, 1))
        if i == 1:
            quadratic()
        if i >= 1:
            finish(i - 1)
    waves(last, (0,))
    finish(last - 1)
    waves(last, (1,))
    finish(last)
    orecv[me] = osend[0]
    for offset in range(1, peers):
        result(offset, False).wait_recv()
    out_ref[...] = jnp.sum(orecv[...], axis=1)
    for copy in started:
        copy.wait_send()


def shards(smatrix, aperture, aberration, beam_k, probe_pos, patches, patch_col):
    peers = lax.axis_size("probe")
    beams, _, width = smatrix.shape
    here = probe_pos.shape[1]
    part = here // lax.axis_size("beam")
    per = patches.shape[0]
    pix = width // 2
    chunks = len(chunk_order(peers))
    overlap = overlap_table(PSIDE)
    vmem = pl.BlockSpec(memory_space=pltpu.VMEM)
    hbm = pl.BlockSpec(memory_space=pl.ANY)
    f32, bf16 = jnp.float32, jnp.bfloat16
    waves = pltpu.VMEM((chunks, 3 * part, width), f32)
    results = pltpu.VMEM((peers, 8, part), f32)
    slots = pltpu.SemaphoreType.DMA((peers,))
    each = pltpu.SemaphoreType.DMA((chunks,))
    return pl.pallas_call(
        functools.partial(kernel, peers),
        out_shape=jax.ShapeDtypeStruct((peers, part), f32),
        in_specs=[hbm] * 8,
        out_specs=vmem,
        scratch_shapes=[
            pltpu.VMEM((beams, width), bf16),
            pltpu.VMEM((2 * beams, width), bf16),
            pltpu.VMEM(overlap.shape, f32),
            pltpu.VMEM((2, beams), f32),
            pltpu.VMEM((2, 4 * part, LANES), f32),
            pltpu.VMEM((peers, 2, here), jnp.int32),
            pltpu.VMEM((peers, 2 * per, pix), bf16),
            pltpu.VMEM((pix, width), bf16),
            waves, waves, waves, results, results,
            pltpu.VMEM((beams // LANES, LANES), f32),
            pltpu.VMEM((beams // LANES, LANES), f32),
            pltpu.VMEM(beam_k.shape, jnp.int32),
            pltpu.VMEM((1, patch_col.shape[0]), jnp.int32),
            pltpu.VMEM(patches.shape, bf16),
            pltpu.SemaphoreType.DMA((6,)),
            pltpu.SemaphoreType.DMA((4,)), pltpu.SemaphoreType.DMA((1,)),
            slots, slots, slots, slots, each, each, slots, slots,
        ],
        compiler_params=pltpu.CompilerParams(
            collective_id=0, has_side_effects=True, vmem_limit_bytes=56 << 20
        ),
    )(
        smatrix.reshape(beams, width),
        aperture.reshape(beams // LANES, LANES),
        aberration.reshape(beams // LANES, LANES),
        beam_k,
        probe_pos,
        patches,
        patch_col.reshape(1, patch_col.shape[0]),
        jnp.asarray(overlap),
    )


def solution(mesh):
    placed = (
        P(("grp", "beam"), "probe", None),
        P("beam"),
        P("beam"),
        P(None, "beam"),
        P(None, "probe"),
        P(("grp", "probe"), None),
        P("grp"),
    )
    whole = jax.shard_map(
        shards, mesh=mesh, in_specs=placed, out_specs=P("grp", ("probe", "beam")), check_vma=False
    )

    def run(*args):
        with jax.sharding.use_abstract_mesh(mesh.abstract_mesh):
            return whole(*args)

    return run
```
